512 devices in a mesh: grp: 8 (over y, x_hi), comp: 64 (over x_lo, z, core).
Axes of the slice: x: 4 (x_hi: 2, x_lo: 2; x = x_hi * 2 + x_lo), y: 4, z: 16, core: 2. Of those that a mesh axis runs over, the one named last changes fastest.
Arguments:
- features: bfloat16 [1048576, 256], P(('grp', 'comp')), may hold values from -8 to 8
- means: float32 [1024, 256], P('comp'), may hold values from -1 to 1
- variances: float32 [1024, 256], P('comp'), may hold values from 0.5 to 2
- weight_logits: float32 [1024], replicated, may hold values from -1 to 1
Outputs:
- new_means: float32 [1024, 256], replicated
- new_variances: float32 [1024, 256], replicated
- new_log_weights: float32 [1024], replicated
- row_scores: float32 [1048576], P(('grp', 'comp'))
The draws below stay inside these ranges and needn't reach their ends.
All inputs are finite; a program needn't handle non-finite values.
Results may differ from the reference program's by a relative error of at most 0.00085.
Values sent between devices are 32-bit elements; how exact they have to be, the bound alone decides.
A program may use at most 64 MiB of HBM per device.

```python
import math
import jax
import jax.numpy as jnp
from jax import lax

K = 1024
D = 256
ROWS_DEV = 2048
ROWS = 1048576


def center_table(key):
    center_key = jax.random.fold_in(key, 11)
    return 0.15 * jnp.clip(jax.random.normal(center_key, (K, D), jnp.float32), -4.0, 4.0)


def draw_features(key, part):
    centers = center_table(key)
    offset_draw = jax.random.randint(jax.random.fold_in(key, 12), (ROWS,), 0, 16)
    block_index = jnp.arange(ROWS, dtype=jnp.int32) // ROWS_DEV
    cluster = (block_index * 2 + offset_draw) % K
    base_rows = centers[cluster]
    noise_key = jax.random.fold_in(key, 13)
    noise = jnp.clip(jax.random.normal(noise_key, (ROWS, D), jnp.float32), -5.0, 5.0)
    values = base_rows + noise
    return values.astype(jnp.bfloat16)


def draw_means(key, part):
    centers = center_table(key)
    shift_key = jax.random.fold_in(key, 15)
    shift = 0.05 * jnp.clip(jax.random.normal(shift_key, (K, D), jnp.float32), -4.0, 4.0)
    return centers + shift


def shard_levels(rng, extent, cuts, least, top_value):
    loudness = 1.0
    for axis_at, parts in cuts:
        heights = jax.random.uniform(jax.random.fold_in(jax.random.fold_in(rng, 6), axis_at), (parts,), jnp.float32, least / len(cuts), top_value / len(cuts))
        loudness = loudness * jnp.repeat(jnp.exp(heights), extent[axis_at] // parts).reshape((-1,) + (1,) * (len(extent) - 1 - axis_at))
    return loudness


def setup_inputs(seed: int = 0) -> dict:
    splits = jax.random.split(jax.random.key(seed), 5)
    return {
        "features": draw_features(jax.random.fold_in(splits[4], 71), 0),
        "means": draw_means(jax.random.fold_in(splits[4], 71), 0),
        "variances": jnp.clip(jnp.exp(math.log(2.0) - 1.3862944 * jax.random.uniform(splits[2], (K, D), jnp.float32) ** shard_levels(splits[2], (K, D), ((0, 64),), -0.2, 0.2)), 0.5, 2.0),
        "weight_logits": jnp.clip(jax.random.uniform(splits[3], (K,), jnp.float32, -1.0, 1.0), -1.0, 1.0),
    }


def update_step(moments, counts, total_rows):
    width = moments.shape[1] // 2
    denominator = (counts + 1.0)[:, None]
    fresh_means = moments[:, :width] / denominator
    fresh_variances = (moments[:, width:] + 1.0) / denominator - fresh_means * fresh_means + 0.01
    fresh_weights = jnp.log((counts + 1.0) / total_rows)
    return fresh_means, fresh_variances, fresh_weights


def reference(features, means, variances, weight_logits):
    inverse = 1.0 / variances
    coefficient = jnp.concatenate([-0.5 * inverse, means * inverse], axis=1)
    offsets = jax.nn.log_softmax(weight_logits) - 0.5 * jnp.sum(jnp.log(variances) + means * means * inverse, axis=1) - 0.5 * D * math.log(2.0 * math.pi)
    blocks = features.reshape(ROWS // ROWS_DEV, ROWS_DEV, D)

    def visit(accumulated, block_rows):
        moments, counts = accumulated
        values = block_rows.astype(jnp.float32)
        squared = values * values
        scores = jnp.dot(jnp.concatenate([squared, values], axis=1), coefficient.T, precision=lax.Precision.HIGHEST) + offsets
        highest = jnp.max(scores, axis=1, keepdims=True)
        exponent = jnp.exp(scores - highest)
        totals = jnp.sum(exponent, axis=1, keepdims=True)
        responsibility = (exponent / totals).astype(jnp.bfloat16)
        block_scores = (highest[:, 0] + jnp.log(totals[:, 0])) / D
        moment_inputs = jnp.concatenate([block_rows, squared.astype(jnp.bfloat16)], axis=1)
        moments = moments + jnp.dot(responsibility.T, moment_inputs, preferred_element_type=jnp.float32)
        counts = counts + jnp.dot(jnp.ones((ROWS_DEV,), jnp.bfloat16), responsibility, preferred_element_type=jnp.float32)
        return (moments, counts), block_scores

    start_state = (jnp.zeros((K, 2 * D), jnp.float32), jnp.zeros((K,), jnp.float32))
    (moments, counts), scores_all = lax.scan(visit, start_state, blocks)
    fresh_means, fresh_variances, fresh_weights = update_step(moments, counts, jnp.float32(ROWS + K))
    return fresh_means, fresh_variances, fresh_weights, scores_all.reshape(ROWS)
```

```python
import functools
import math

import jax
import jax.numpy as jnp
from jax import lax
from jax.experimental import pallas as pl
from jax.experimental.pallas import tpu as pltpu
from jax.sharding import PartitionSpec as P

MESH = pl.DeviceIdType.MESH
VMEM = pl.BlockSpec(memory_space=pltpu.VMEM)
BF16 = jnp.bfloat16
F32 = jnp.float32

XA, XB, YA, YB = 0, 1, 2, 3
ORDERS = ((XA, XB, YA, YB), (XB, XA, YB, YA), (YA, YB, XA, XB), (YB, YA, XB, XA))
STREAMS = 4
DEPTH = 16


def chunk_bits(y_hi, y_lo, u, v):
    return ((u + v) % 2, u, (y_hi + y_lo) % 2, y_hi)


def place():
    grp = lax.axis_index("grp")
    comp = lax.axis_index("comp")
    y, u = lax.div(grp, 2), lax.rem(grp, 2)
    v, z, core = lax.div(comp, 32), lax.rem(lax.div(comp, 2), DEPTH), lax.rem(comp, 2)
    y_hi, y_lo = lax.div(y, 2), lax.rem(y, 2)
    bits = (lax.rem(u + v, 2), u, lax.rem(y_hi + y_lo, 2), y_hi)
    flip_v = comp + 32 - 64 * v
    partners = (
        (grp, flip_v),
        (grp + 1 - 2 * u, flip_v),
        (2 * (y + 1 - 2 * y_lo) + u, comp),
        (2 * (3 - y) + u, comp),
    )
    sibling = (grp, comp + 1 - 2 * core)

    def along_z(step):
        return (grp, 32 * v + 2 * lax.rem(z + step, DEPTH) + core)

    return grp, z, core, bits, partners, sibling, along_z


def greet(partners, sibling, along_z):
    barrier = pltpu.get_barrier_semaphore()
    peers = [*partners, sibling, *(along_z(step) for step in range(1, DEPTH))]
    for peer in peers:
        pl.semaphore_signal(barrier, inc=1, device_id=peer, device_id_type=MESH)
    pl.semaphore_wait(barrier, len(peers))


def send(source, target, sems, at, peer):
    copy = pltpu.make_async_remote_copy(
        src_ref=source,
        dst_ref=target,
        send_sem=sems.at[(0, *at)],
        recv_sem=sems.at[(1, *at)],
        device_id=peer,
        device_id_type=MESH,
    )
    copy.start()
    return copy


def gather_kernel(means_ref, variances_ref, out_ref, tiles, arrived, z_sems, plane_sems, core_sems):
    grp, z, core, bits, partners, sibling, along_z = place()
    for index in range(8):
        source = means_ref if index < 4 else variances_ref
        column, row = (index // 2) % 2, index % 2
        tiles[index] = source[row * 8 : row * 8 + 8, column * 128 : column * 128 + 128]
    greet(partners, sibling, along_z)
    copies = [
        send(tiles.at[grp], arrived.at[z], z_sems, (step,), along_z(step))
        for step in range(1, DEPTH)
    ]
    arrived[z] = tiles[grp]
    for copy in copies:
        copy.wait()
    starts = []
    for stream, order in enumerate(ORDERS):
        own = core * 16
        for level, direction in enumerate(order):
            own = own + bits[direction] * (8 >> level)
        starts.append(own)
        for slot in range(4):
            out_ref[stream, own, slot] = arrived[stream * 4 + slot]
    shared = []
    pending = [None] * STREAMS
    for level in range(5):
        for stream, order in enumerate(ORDERS):
            size = 1 << level
            if level > 0:
                pending[stream].wait()
                fresh_bit = bits[order[4 - level]]
                half = size // 2
                fresh = starts[stream] + (1 - 2 * fresh_bit) * half
                starts[stream] = starts[stream] - fresh_bit * half
            else:
                half, fresh = 1, starts[stream]
            if level < 4:
                direction = order[3 - level]
                held = out_ref.at[stream, pl.ds(starts[stream], size)]
                pending[stream] = send(held, held, plane_sems, (level, stream), partners[direction])
            held = out_ref.at[stream, pl.ds(fresh, half)]
            shared.append(send(held, held, core_sems, (level, stream), sibling))
    for copy in shared:
        copy.wait()


def gather(means, variances):
    return pl.pallas_call(
        gather_kernel,
        out_shape=jax.ShapeDtypeStruct((STREAMS, 32, 4, 8, 128), F32),
        in_specs=[VMEM, VMEM],
        out_specs=VMEM,
        scratch_shapes=[
            pltpu.VMEM((8, 8, 128), F32),
            pltpu.VMEM((DEPTH, 8, 128), F32),
            pltpu.SemaphoreType.DMA((2, DEPTH)),
            pltpu.SemaphoreType.DMA((2, 4, STREAMS)),
            pltpu.SemaphoreType.DMA((2, 5, STREAMS)),
        ],
        compiler_params=pltpu.CompilerParams(
            collective_id=0, has_side_effects=True, vmem_limit_bytes=16 << 20
        ),
    )(means, variances)


def stats_kernel(
    parameters_ref, features_ref, logits_ref, moments_ref, counts_ref, rows_ref,
    weights, offsets, inputs, scores, shares, sums,
):
    total_comps, width = 1024, 256
    local_rows = features_ref.shape[0]
    block = 256
    logits = logits_ref[...]
    top = jnp.max(logits)
    log_weights = logits - top - jnp.log(jnp.sum(jnp.exp(logits - top)))
    for piece in range(8):
        spread = jnp.broadcast_to(log_weights[piece : piece + 1, :], (128, 128))
        offsets[piece * 128 : piece * 128 + 128, :] = jnp.transpose(spread)

    for v in range(2):
        for z in range(DEPTH):
            for core in range(2):
                first = 16 * (32 * v + 2 * z + core)
                rows = slice(first, first + 16)
                order = ORDERS[z // 4]

                def table(kind, column):
                    pieces = []
                    for u in range(2):
                        bits = chunk_bits(kind, column, u, v)
                        index = core * 16
                        for level, direction in enumerate(order):
                            index = index + bits[direction] * (8 >> level)
                        pieces.append(parameters_ref[z // 4, index, z % 4])
                    return jnp.concatenate(pieces, axis=0)

                penalty = None
                for column in range(2):
                    mean, variance = table(0, column), table(1, column)
                    inverse = 1.0 / variance
                    square_part = -0.5 * inverse
                    linear_part = mean * inverse
                    term = jnp.log(variance) + mean * linear_part
                    penalty = term if penalty is None else penalty + term
                    square_high = square_part.astype(BF16)
                    square_low = (square_part - square_high.astype(F32)).astype(BF16)
                    linear_high = linear_part.astype(BF16)
                    linear_low = (linear_part - linear_high.astype(F32)).astype(BF16)
                    for place_at, value in enumerate(
                        (square_high, square_high, square_low, linear_high, linear_low)
                    ):
                        at = place_at * width + column * 128
                        weights[rows, at : at + 128] = value
                penalty = jnp.sum(penalty, axis=1, keepdims=True)
                offsets[rows, :] = (
                    offsets[rows, :] - 0.5 * penalty - 0.5 * width * math.log(2.0 * math.pi)
                )

    sums[...] = jnp.zeros_like(sums)

    def visit(step, carry):
        at = pl.multiple_of(step * block, block)
        x = features_ref[pl.ds(at, block), :]
        values = x.astype(F32)
        squared = values * values
        high = squared.astype(BF16)
        low = (squared - high.astype(F32)).astype(BF16)
        inputs[pl.ds(at, block), :width] = x
        inputs[pl.ds(at, block), width:] = high
        right = jnp.concatenate([high, low, high, x, x], axis=1)
        best = None
        for part in range(0, total_comps, 256):
            raw = lax.dot_general(
                weights[part : part + 256, :], right, (((1,), (1,)), ((), ())),
                preferred_element_type=F32,
            )
            offset = offsets[part : part + 256, :]
            raw = raw + jnp.concatenate([offset, offset], axis=1)
            scores[part : part + 256, :] = raw
            here = jnp.max(raw, axis=0, keepdims=True)
            best = here if best is None else jnp.maximum(best, here)
        totals = None
        for part in range(0, total_comps, 256):
            exponent = jnp.exp(scores[part : part + 256, :] - best)
            scores[part : part + 256, :] = exponent
            here = jnp.sum(exponent, axis=0, keepdims=True)
            totals = here if totals is None else totals + here
        rows_ref[:, pl.ds(at, block)] = (best + jnp.log(totals)) / width
        scale = 1.0 / totals
        for part in range(0, total_comps, 256):
            share = (scores[part : part + 256, :] * scale).astype(BF16)
            shares[part : part + 256, pl.ds(at, block)] = share
            rounded = share.astype(F32)
            sums[part : part + 256, :] += rounded[:, :128] + rounded[:, 128:]
        return carry

    lax.fori_loop(0, local_rows // block, visit, 0)
    for part in range(0, total_comps, 256):
        moments_ref[part : part + 256, :] = jnp.dot(
            shares[part : part + 256, :], inputs[...], preferred_element_type=F32
        )
    for piece in range(8):
        turned = jnp.transpose(sums[piece * 128 : piece * 128 + 128, :])
        counts_ref[piece : piece + 1, :] = jnp.sum(turned, axis=0, keepdims=True)


def stats(parameters, features, logits):
    rows = features.shape[0]
    return pl.pallas_call(
        stats_kernel,
        out_shape=(
            jax.ShapeDtypeStruct((1024, 512), F32),
            jax.ShapeDtypeStruct((8, 128), F32),
            jax.ShapeDtypeStruct((1, rows), F32),
        ),
        in_specs=[VMEM] * 3,
        out_specs=(VMEM,) * 3,
        scratch_shapes=[
            pltpu.VMEM((1024, 1280), BF16),
            pltpu.VMEM((1024, 128), F32),
            pltpu.VMEM((rows, 512), BF16),
            pltpu.VMEM((1024, 256), F32),
            pltpu.VMEM((1024, rows), BF16),
            pltpu.VMEM((1024, 128), F32),
        ],
        compiler_params=pltpu.CompilerParams(vmem_limit_bytes=40 << 20),
    )(parameters, features, logits)


def reduce_kernel(
    moments_ref, counts_ref, out_ref, counts_out_ref,
    kept, core_in, in_0, in_1, in_2, in_3, mine, z_in, z_out, counts_z, counts_in, counts_now,
    core_sems, plane_sems, z_sems, back_z_sems, back_plane_sems, back_core_sems,
    counts_z_sems, counts_sems,
):
    grp, z, core, bits, partners, sibling, along_z = place()
    plane_in = (in_0, in_1, in_2, in_3)
    half_comps = 512
    greet(partners, sibling, along_z)
    core_copies = []
    for stream in range(STREAMS):
        source = moments_ref.at[pl.ds((1 - core) * half_comps + stream * 128, 128)]
        core_copies.append(send(source, core_in.at[stream], core_sems, (stream,), sibling))
    counts_copies = [
        send(counts_ref, counts_z.at[z], counts_z_sems, (step,), along_z(step))
        for step in range(1, DEPTH)
    ]
    counts_z[z] = counts_ref[...]

    starts = [[0] * STREAMS]
    pending = [None] * STREAMS

    def advance(level):
        half = 64 >> level
        for stream, order in enumerate(ORDERS):
            start = starts[level][stream]
            bit = bits[order[level]]
            source = kept.at[stream, pl.ds(start + (1 - bit) * half, half)]
            pending[stream] = send(
                source, plane_in[level].at[stream], plane_sems, (level, stream),
                partners[order[level]],
            )

    for stream in range(STREAMS):
        core_copies[stream].wait()
        kept[stream] = (
            moments_ref[pl.ds(core * half_comps + stream * 128, 128), :] + core_in[stream]
        )
    advance(0)
    for copy in counts_copies:
        copy.wait()
    total = counts_z[0]
    for index in range(1, DEPTH):
        total = total + counts_z[index]
    counts_now[0] = total
    routes = (sibling, *partners)

    def count_start(level):
        return send(counts_now.at[level], counts_in.at[level], counts_sems, (level,), routes[level])

    def count_end(level, copy):
        copy.wait()
        counts_now[level + 1] = counts_now[level] + counts_in[level]

    counting = count_start(0)
    for level in range(4):
        half = 64 >> level
        following = []
        for stream, order in enumerate(ORDERS):
            pending[stream].wait()
            keep = starts[level][stream] + bits[order[level]] * half
            kept[stream, pl.ds(keep, half), :] = (
                kept[stream, pl.ds(keep, half), :] + plane_in[level][stream]
            )
            following.append(keep)
        starts.append(following)
        if level < 3:
            advance(level + 1)
        count_end(level, counting)
        counting = count_start(level + 1)
    for stream in range(STREAMS):
        for column in range(4):
            mine[stream * 4 + column] = kept[
                stream, pl.ds(starts[4][stream], 8), column * 128 : column * 128 + 128
            ]
    copies = [
        send(mine.at[lax.rem(z + step, DEPTH)], z_in.at[step], z_sems, (step,), along_z(step))
        for step in range(1, DEPTH)
    ]
    count_end(4, counting)
    counts_out_ref[...] = counts_now[5]
    tile = mine[z]
    for step, copy in enumerate(copies):
        copy.wait()
        tile = tile + z_in[step + 1]
    z_out[z] = tile
    copies = [
        send(z_out.at[z], z_out.at[z], back_z_sems, (step,), along_z(step))
        for step in range(1, DEPTH)
    ]
    for copy in copies:
        copy.wait()
    for stream in range(STREAMS):
        first = core * half_comps + stream * 128 + starts[4][stream]
        for column in range(4):
            out_ref[pl.ds(first, 8), column * 128 : column * 128 + 128] = z_out[stream * 4 + column]
    shared = []
    for level in range(4, -1, -1):
        size = 128 >> level
        for stream, order in enumerate(ORDERS):
            base = core * half_comps + stream * 128
            if level < 4:
                pending[stream].wait()
                fresh = starts[level][stream] + (1 - bits[order[level]]) * (size // 2)
                fresh_size = size // 2
            else:
                fresh, fresh_size = starts[4][stream], size
            if level > 0:
                held = out_ref.at[pl.ds(base + starts[level][stream], size)]
                pending[stream] = send(
                    held, held, back_plane_sems, (level - 1, stream), partners[order[level - 1]]
                )
            held = out_ref.at[pl.ds(base + fresh, fresh_size)]
            shared.append(send(held, held, back_core_sems, (level, stream), sibling))
    for copy in shared:
        copy.wait()


def reduce_all(moments, counts):
    dma = pltpu.SemaphoreType.DMA
    return pl.pallas_call(
        reduce_kernel,
        out_shape=(
            jax.ShapeDtypeStruct((1024, 512), F32),
            jax.ShapeDtypeStruct((8, 128), F32),
        ),
        in_specs=[VMEM, VMEM],
        out_specs=(VMEM, VMEM),
        scratch_shapes=[
            pltpu.VMEM((STREAMS, 128, 512), F32),
            pltpu.VMEM((STREAMS, 128, 512), F32),
            pltpu.VMEM((STREAMS, 64, 512), F32),
            pltpu.VMEM((STREAMS, 32, 512), F32),
            pltpu.VMEM((STREAMS, 16, 512), F32),
            pltpu.VMEM((STREAMS, 8, 512), F32),
            pltpu.VMEM((DEPTH, 8, 128), F32),
            pltpu.VMEM((DEPTH, 8, 128), F32),
            pltpu.VMEM((DEPTH, 8, 128), F32),
            pltpu.VMEM((DEPTH, 8, 128), F32),
            pltpu.VMEM((5, 8, 128), F32),
            pltpu.VMEM((6, 8, 128), F32),
            dma((2, STREAMS)),
            dma((2, 4, STREAMS)),
            dma((2, DEPTH)),
            dma((2, DEPTH)),
            dma((2, 4, STREAMS)),
            dma((2, 5, STREAMS)),
            dma((2, DEPTH)),
            dma((2, 5)),
        ],
        compiler_params=pltpu.CompilerParams(
            collective_id=1, has_side_effects=True, vmem_limit_bytes=24 << 20
        ),
    )(moments, counts)


def update_step(moments, counts, total_rows):
    width = moments.shape[1] // 2
    denominator = (counts + 1.0)[:, None]
    fresh_means = moments[:, :width] / denominator
    fresh_variances = (moments[:, width:] + 1.0) / denominator - fresh_means * fresh_means + 0.01
    fresh_weights = jnp.log((counts + 1.0) / total_rows)
    return (fresh_means, fresh_variances, fresh_weights)


def on_device(features, means, variances, weight_logits):
    parameters = gather(means, variances)
    moments, counts, row_scores = stats(parameters, features, weight_logits.reshape(8, 128))
    moments, counts = reduce_all(moments, counts)
    total_comps = moments.shape[0]
    total_rows = jnp.float32(
        features.shape[0] * lax.axis_size("grp") * lax.axis_size("comp") + total_comps
    )
    fresh = update_step(moments, counts.reshape(total_comps), total_rows)
    return (*fresh, row_scores.reshape(features.shape[0]))


def solution(mesh):
    return jax.shard_map(
        on_device,
        mesh=mesh,
        in_specs=(P(("grp", "comp"), None), P("comp", None), P("comp", None), P()),
        out_specs=(P(), P(), P(), P(("grp", "comp"))),
        check_vma=False,
    )
```

```python
import math

import jax
import jax.numpy as jnp
from jax import lax
from jax.experimental import pallas as pl
from jax.experimental.pallas import tpu as pltpu
from jax.sharding import PartitionSpec as P

MESH = pl.DeviceIdType.MESH
BF16 = jnp.bfloat16
F32 = jnp.float32

COMPS, WIDTH = 1024, 256
DEPTH = 16
OFFSETS = sorted(
    ((dx, dy) for dx in range(4) for dy in range(4) if (dx, dy) != (0, 0)),
    key=lambda d: (min(d[0], 4 - d[0]) + min(d[1], 4 - d[1]), d),
)
PEERS = len(OFFSETS)
SHIFTS = (0, 1, 3, 2)
GROUPS = len(SHIFTS)
FAR_FIRST = (3, 1, 2, 0)
BLOCK = 256


class Place:
    def __init__(self):
        self.grp = lax.axis_index("grp")
        comp = lax.axis_index("comp")
        y, u = lax.div(self.grp, 2), lax.rem(self.grp, 2)
        v, rest = lax.div(comp, 32), lax.rem(comp, 32)
        self.z, self.core = lax.div(rest, 2), lax.rem(rest, 2)
        self.block, self.slot = lax.div(self.z, 4), lax.rem(self.z, 4)
        self.chip = 2 * self.grp + v
        self.sibling = (self.grp, comp + 1 - 2 * self.core)
        self.base = 32 * v + self.core
        x = 2 * u + v
        self.plane = []
        for dx, dy in OFFSETS:
            across, along = lax.rem(x + dx, 4), lax.rem(y + dy, 4)
            grp = 2 * along + lax.div(across, 2)
            side = lax.rem(across, 2)
            self.plane.append(((grp, 32 * side + rest), 2 * grp + side))

    def at_z(self, z):
        return (self.grp, self.base + 2 * z)

    def group(self, index):
        return lax.rem(self.block + SHIFTS[index], 4)


def remote(source, target, send_sem, recv_sem, peer):
    return pltpu.make_async_remote_copy(
        src_ref=source, dst_ref=target, send_sem=send_sem, recv_sem=recv_sem,
        device_id=peer, device_id_type=MESH,
    )


def await_bytes(ref, sem):
    pltpu.make_async_copy(ref, ref, sem).wait()


def kernel(
    features_hbm, means_hbm, variances_hbm, logits_ref,
    moments_ref, counts_ref, rows_ref,
    features, means, variances, tiles, arrived, table, weights, log_weights, inputs,
    exponents, peaks, totals, shares, tally,
    core_out, core_in, own, plane_in, z_out, z_in, back, spread,
    counts_z, counts_plane, counts_pair,
    load_sems, z_send, z_recv, plane_send, plane_recv, pair_send, pair_recv,
    rz_send, rz_recv, rplane_send, rplane_recv, rpair_send, rpair_recv,
    bz_send, bz_recv, bplane_send, bplane_recv, bpair_send, bpair_recv,
    count_send, count_recv,
):
    me = Place()
    local_rows = features.shape[0]
    loads = [
        pltpu.make_async_copy(source, target, load_sems.at[index])
        for index, (source, target) in enumerate(
            ((means_hbm, means), (variances_hbm, variances), (features_hbm, features))
        )
    ]
    for load in loads:
        load.start()
    barrier = pltpu.get_barrier_semaphore()
    greeted = [me.at_z(lax.rem(me.z + step, DEPTH)) for step in range(1, DEPTH)]
    greeted += [peer for peer, _ in me.plane] + [me.sibling]
    for peer in greeted:
        pl.semaphore_signal(barrier, inc=1, device_id=peer, device_id_type=MESH)
    loads[0].wait()
    loads[1].wait()
    for index in range(8):
        source = means if index < 4 else variances
        column, row = (index // 2) % 2, index % 2
        tiles[index] = source[row * 8 : row * 8 + 8, column * 128 : column * 128 + 128]
    arrived[me.z] = tiles[me.grp]
    pl.semaphore_wait(barrier, len(greeted))

    z_steps = (8, 7, 9, 6, 10, 5, 11, 4, 12, 3, 13, 2, 14, 1, 15)
    for step in z_steps:
        remote(
            tiles.at[me.grp], arrived.at[me.z], z_send.at[0], z_recv.at[me.block],
            me.at_z(lax.rem(me.z + step, DEPTH)),
        ).start()

    logits = logits_ref[...]
    top = jnp.max(logits)
    normal = logits - top - jnp.log(jnp.sum(jnp.exp(logits - top)))
    for piece in range(8):
        wide = jnp.broadcast_to(normal[piece : piece + 1, :], (128, 128))
        log_weights[piece * 128 : piece * 128 + 128, :] = jnp.transpose(wide)
    loads[2].wait()

    def prepare(step, carry):
        at = pl.multiple_of(step * 128, 128)
        x = features[pl.ds(at, 128), :]
        values = x.astype(F32)
        squared = values * values
        high = squared.astype(BF16)
        low = (squared - high.astype(F32)).astype(BF16)
        for index, value in enumerate((high, low, high, x, x)):
            inputs[pl.ds(at, 128), index * WIDTH : index * WIDTH + WIDTH] = value
        return carry

    lax.fori_loop(0, local_rows // 128, prepare, 0)

    def await_group(buffer, sems, index):
        count = 3 if index == 0 else 4
        await_bytes(buffer.at[pl.ds(0, count)], sems.at[me.group(index)])

    for index in range(GROUPS):
        await_group(arrived, z_recv, index)
        first = 4 * me.group(index)
        table[index, me.core, me.chip] = arrived[pl.ds(first, 4)]
        for offset, (peer, _) in enumerate(me.plane):
            remote(
                arrived.at[pl.ds(first, 4)], table.at[index, me.core, me.chip],
                plane_send.at[index], plane_recv.at[index], peer,
            ).start()

    def pair_copy(index):
        part = table.at[index, me.core]
        return remote(part, part, pair_send.at[index], pair_recv.at[index], me.sibling)

    def make_weights(index):
        natural = 128 * me.group(index)
        for v in range(2):
            for j in range(4):
                for h in range(2):
                    def load(kind, column):
                        chips = [2 * (4 * kind + 2 * column + r) + v for r in range(2)]
                        return jnp.concatenate([table[index, h, chip, j] for chip in chips], axis=0)

                    inner = 32 * j + 16 * h
                    row = 128 * v + inner
                    rows = slice(row, row + 16)
                    penalty = None
                    for column in range(2):
                        mean, variance = load(0, column), load(1, column)
                        inverse = 1.0 / variance
                        square_part = -0.5 * inverse
                        linear_part = mean * inverse
                        term = jnp.log(variance) + mean * linear_part
                        penalty = term if penalty is None else penalty + term
                        square_high = square_part.astype(BF16)
                        square_low = (square_part - square_high.astype(F32)).astype(BF16)
                        linear_high = linear_part.astype(BF16)
                        linear_low = (linear_part - linear_high.astype(F32)).astype(BF16)
                        for at, value in enumerate(
                            (square_high, square_high, square_low, linear_high, linear_low)
                        ):
                            at = at * WIDTH + column * 128
                            weights[index, rows, at : at + 128] = value
                    penalty = jnp.sum(penalty, axis=1, keepdims=True)
                    here = pl.ds(pl.multiple_of(512 * v + natural + inner, 16), 16)
                    log_weights[here, :] = (
                        log_weights[here, :] - 0.5 * penalty - 0.5 * WIDTH * math.log(2.0 * math.pi)
                    )

    def make_scores(index):
        natural = 128 * me.group(index)

        def visit(step, carry):
            at = pl.multiple_of(step * BLOCK, BLOCK)
            right = inputs[pl.ds(at, BLOCK), :]
            raws = []
            for v in range(2):
                raw = lax.dot_general(
                    weights[index, v * 128 : v * 128 + 128, :], right, (((1,), (1,)), ((), ())),
                    preferred_element_type=F32,
                )
                offset = log_weights[pl.ds(pl.multiple_of(512 * v + natural, 128), 128), :]
                raws.append(raw + jnp.concatenate([offset] * (BLOCK // 128), axis=1))
            best = jnp.max(jnp.maximum(raws[0], raws[1]), axis=0, keepdims=True)
            total = None
            for v in range(2):
                value = jnp.exp(raws[v] - best)
                exponents[index, v, :, pl.ds(at, BLOCK)] = value
                total = value if total is None else total + value
            peaks[index : index + 1, pl.ds(at, BLOCK)] = best
            totals[index : index + 1, pl.ds(at, BLOCK)] = jnp.sum(total, axis=0, keepdims=True)
            return carry

        lax.fori_loop(0, local_rows // BLOCK, visit, 0)

    for index in range(GROUPS):
        await_bytes(table.at[index, 0, pl.ds(0, PEERS)], plane_recv.at[index])
        copy = pair_copy(index)
        copy.start()
        copy.wait_recv()
        make_weights(index)
        make_scores(index)

    best = jnp.max(peaks[0:GROUPS, :], axis=0, keepdims=True)
    factors = jnp.exp(peaks[0:GROUPS, :] - best)
    total = jnp.sum(totals[0:GROUPS, :] * factors, axis=0, keepdims=True)
    rows_ref[...] = (best + jnp.log(total)) / WIDTH
    totals[0:GROUPS, :] = factors / total

    def rpair_copy(index):
        return remote(
            core_out.at[index], core_in.at[index], rpair_send.at[index], rpair_recv.at[index],
            me.sibling,
        )

    for index in FAR_FIRST:
        def share(step, sums):
            at = pl.multiple_of(step * BLOCK, BLOCK)
            scale = totals[index : index + 1, pl.ds(at, BLOCK)]
            following = []
            for v in range(2):
                rounded = (exponents[index, v, :, pl.ds(at, BLOCK)] * scale).astype(BF16)
                shares[index, v, :, pl.ds(at, BLOCK)] = rounded
                wide = rounded.astype(F32)
                tally[v] += wide[:, :128] + wide[:, 128:]
            return sums

        tally[...] = jnp.zeros_like(tally)
        lax.fori_loop(0, local_rows // BLOCK, share, 0)
        for v in range(2):
            line = jnp.sum(jnp.transpose(tally[v]), axis=0, keepdims=True)
            counts_pair[0, pl.ds(4 * v + me.group(index), 1), :] = line
        for target, half in ((core_out, 1 - me.core), (own, me.core)):
            result = jnp.dot(
                shares[index, half], inputs[:, 2 * WIDTH : 4 * WIDTH], preferred_element_type=F32
            )
            for chip in range(16):
                for j in range(4):
                    target[index, chip, j] = result[
                        chip * 8 : chip * 8 + 8, j * 128 : j * 128 + 128
                    ]
            if target is core_out:
                rpair_copy(index).start()
        rpair_copy(index).wait_recv()
        own[index] = own[index] + core_in[index]
        for offset, (peer, chip) in enumerate(me.plane):
            remote(
                own.at[index, chip], plane_in.at[index, offset],
                rplane_send.at[index], rplane_recv.at[index], peer,
            ).start()

    for step in z_steps:
        remote(
            counts_pair.at[0], counts_z.at[me.z], count_send.at[0], count_recv.at[0],
            me.at_z(lax.rem(me.z + step, DEPTH)),
        ).start()
    counts_z[me.z] = counts_pair[0]

    for index in FAR_FIRST:
        await_bytes(plane_in.at[index], rplane_recv.at[index])
        reduced = own[index, me.chip]
        for offset in range(PEERS):
            reduced = reduced + plane_in[index, offset]
        z_out[index] = reduced
        for step in range(1 if index == 0 else 0, 4):
            slot = lax.rem(me.slot + step, 4)
            remote(
                z_out.at[index, slot], z_in.at[me.z], rz_send.at[0], rz_recv.at[0],
                me.at_z(4 * me.group(index) + slot),
            ).start()
    z_in[me.z] = z_out[0, me.slot]

    await_bytes(counts_z.at[pl.ds(0, DEPTH - 1)], count_recv.at[0])
    counted = counts_z[0]
    for index in range(1, DEPTH):
        counted = counted + counts_z[index]
    counts_plane[me.chip] = counted
    for peer, _ in me.plane:
        remote(
            counts_plane.at[me.chip], counts_plane.at[me.chip], count_send.at[1], count_recv.at[1],
            peer,
        ).start()

    await_bytes(z_in.at[pl.ds(0, DEPTH - 1)], rz_recv.at[0])
    final = z_in[0]
    for index in range(1, DEPTH):
        final = final + z_in[index]
    back[me.z] = final
    for step in z_steps:
        remote(
            back.at[me.z], back.at[me.z], bz_send.at[0], bz_recv.at[me.block],
            me.at_z(lax.rem(me.z + step, DEPTH)),
        ).start()

    await_bytes(counts_plane.at[pl.ds(0, PEERS)], count_recv.at[1])
    counted = counts_plane[0]
    for index in range(1, 16):
        counted = counted + counts_plane[index]
    counts_pair[1] = counted
    pair = remote(
        counts_pair.at[1], counts_pair.at[2], count_send.at[2], count_recv.at[2], me.sibling
    )
    pair.start()

    for index in range(GROUPS):
        await_group(back, bz_recv, index)
        first = 4 * me.group(index)
        spread[index, me.core, me.chip] = back[pl.ds(first, 4)]
        for peer, _ in me.plane:
            remote(
                back.at[pl.ds(first, 4)], spread.at[index, me.core, me.chip],
                bplane_send.at[index], bplane_recv.at[index], peer,
            ).start()

    pair.wait()
    counts_ref[...] = counts_pair[1] + counts_pair[2]

    await_bytes(arrived.at[pl.ds(0, DEPTH - 1)], z_send.at[0])
    await_bytes(counts_z.at[pl.ds(0, DEPTH - 1)], count_send.at[0])
    await_bytes(counts_z.at[pl.ds(0, DEPTH - 1)], count_send.at[1])
    await_bytes(z_in.at[pl.ds(0, DEPTH - 1)], rz_send.at[0])
    await_bytes(z_in.at[pl.ds(0, DEPTH - 1)], bz_send.at[0])
    for index in range(GROUPS):
        await_bytes(plane_in.at[index], plane_send.at[index])
        await_bytes(plane_in.at[index], rplane_send.at[index])
        pair_copy(index).wait_send()
        rpair_copy(index).wait_send()

    def bpair_copy(index):
        part = spread.at[index, me.core]
        return remote(part, part, bpair_send.at[index], bpair_recv.at[index], me.sibling)

    for index in range(GROUPS):
        await_bytes(spread.at[index, 0, pl.ds(0, PEERS)], bplane_recv.at[index])
        bpair_copy(index).start()
    for index in range(GROUPS):
        bpair_copy(index).wait_recv()
        natural = 128 * me.group(index)
        for h in range(2):
            for chip in range(16):
                here = pl.ds(pl.multiple_of(512 * h + natural + 8 * chip, 8), 8)
                for j in range(4):
                    moments_ref[here, j * 128 : j * 128 + 128] = spread[index, h, chip, j]
    for index in range(GROUPS):
        await_bytes(plane_in.at[index], bplane_send.at[index])
        bpair_copy(index).wait_send()


def iterate(features, means, variances, logits):
    rows = features.shape[0]
    dma = pltpu.SemaphoreType.DMA
    hbm = pl.BlockSpec(memory_space=pl.ANY)
    vmem = pl.BlockSpec(memory_space=pltpu.VMEM)
    tile = (8, 128)
    return pl.pallas_call(
        kernel,
        out_shape=(
            jax.ShapeDtypeStruct((COMPS, 2 * WIDTH), F32),
            jax.ShapeDtypeStruct(tile, F32),
            jax.ShapeDtypeStruct((1, rows), F32),
        ),
        in_specs=[hbm, hbm, hbm, vmem],
        out_specs=(vmem,) * 3,
        scratch_shapes=[
            pltpu.VMEM((rows, WIDTH), BF16),
            pltpu.VMEM((16, WIDTH), F32),
            pltpu.VMEM((16, WIDTH), F32),
            pltpu.VMEM((8, *tile), F32),
            pltpu.VMEM((DEPTH, *tile), F32),
            pltpu.VMEM((GROUPS, 2, 16, 4, *tile), F32),
            pltpu.VMEM((GROUPS, 256, 5 * WIDTH), BF16),
            pltpu.VMEM((COMPS, 128), F32),
            pltpu.VMEM((rows, 5 * WIDTH), BF16),
            pltpu.VMEM((GROUPS, 2, 128, rows), F32),
            pltpu.VMEM((8, rows), F32),
            pltpu.VMEM((8, rows), F32),
            pltpu.VMEM((GROUPS, 2, 128, rows), BF16),
            pltpu.VMEM((2, 128, 128), F32),
            pltpu.VMEM((GROUPS, 16, 4, *tile), F32),
            pltpu.VMEM((GROUPS, 16, 4, *tile), F32),
            pltpu.VMEM((GROUPS, 16, 4, *tile), F32),
            pltpu.VMEM((GROUPS, PEERS, 4, *tile), F32),
            pltpu.VMEM((GROUPS, 4, *tile), F32),
            pltpu.VMEM((DEPTH, *tile), F32),
            pltpu.VMEM((DEPTH, *tile), F32),
            pltpu.VMEM((GROUPS, 2, 16, 4, *tile), F32),
            pltpu.VMEM((DEPTH, *tile), F32),
            pltpu.VMEM((16, *tile), F32),
            pltpu.VMEM((3, *tile), F32),
            dma((3,)),
            dma((1,)), dma((4,)), dma((4,)), dma((4,)), dma((4,)), dma((4,)),
            dma((1,)), dma((1,)), dma((4,)), dma((4,)), dma((4,)), dma((4,)),
            dma((1,)), dma((4,)), dma((4,)), dma((4,)), dma((4,)), dma((4,)),
            dma((3,)), dma((3,)),
        ],
        compiler_params=pltpu.CompilerParams(
            collective_id=0, has_side_effects=True, vmem_limit_bytes=56 << 20
        ),
    )(features, means, variances, logits)


def update_step(squares, linears, counts, total_rows):
    denominator = (counts + 1.0)[:, None]
    fresh_means = linears / denominator
    fresh_variances = (squares + 1.0) / denominator - fresh_means * fresh_means + 0.01
    fresh_weights = jnp.log((counts + 1.0) / total_rows)
    return (fresh_means, fresh_variances, fresh_weights)


def on_device(features, means, variances, weight_logits):
    moments, counts, row_scores = iterate(
        features, means, variances, weight_logits.reshape(8, 128)
    )
    total_rows = jnp.float32(
        features.shape[0] * lax.axis_size("grp") * lax.axis_size("comp") + COMPS
    )
    fresh = update_step(
        moments[:, :WIDTH], moments[:, WIDTH:], counts.reshape(COMPS), total_rows
    )
    return (*fresh, row_scores.reshape(features.shape[0]))


def solution(mesh):
    return jax.shard_map(
        on_device,
        mesh=mesh,
        in_specs=(P(("grp", "comp"), None), P("comp", None), P("comp", None), P()),
        out_specs=(P(), P(), P(), P(("grp", "comp"))),
        check_vma=False,
    )
```

```python
import functools
import math

import jax
import jax.numpy as jnp
from jax import lax
from jax.experimental import pallas as pl
from jax.experimental.pallas import tpu as pltpu
from jax.sharding import PartitionSpec as P

MESH = pl.DeviceIdType.MESH
BF16 = jnp.bfloat16
F32 = jnp.float32

COMPS, WIDTH = 1024, 256
DEPTH = 16
OFFSETS = sorted(
    ((dx, dy) for dx in range(4) for dy in range(4) if (dx, dy) != (0, 0)),
    key=lambda d: (min(d[0], 4 - d[0]) + min(d[1], 4 - d[1]), d),
)
PEERS = len(OFFSETS)
NEAR = (0, 1, -1, 2, -2, 3, -3, 4, -4, 5, -5, 6, -6, 7, -7, 8)
SLOT = {step % DEPTH: slot for slot, step in enumerate(NEAR)}
HOPS = ((0, 1), (1, 3), (4, 2), (6, 2), (8, 2), (10, 2), (12, 2), (14, 2))
HOP_OF = {first + k: hop for hop, (first, count) in enumerate(HOPS) for k in range(count)}
GROUPS = 4
BLOCK = 256


class Place:
    def __init__(self):
        self.grp = lax.axis_index("grp")
        comp = lax.axis_index("comp")
        y, u = lax.div(self.grp, 2), lax.rem(self.grp, 2)
        v, rest = lax.div(comp, 32), lax.rem(comp, 32)
        self.z, self.core = lax.div(rest, 2), lax.rem(rest, 2)
        self.chip = 2 * self.grp + v
        self.sibling = (self.grp, comp + 1 - 2 * self.core)
        self.base = 32 * v + self.core
        x = 2 * u + v
        self.plane = []
        for dx, dy in OFFSETS:
            across, along = lax.rem(x + dx, 4), lax.rem(y + dy, 4)
            grp = 2 * along + lax.div(across, 2)
            side = lax.rem(across, 2)
            self.plane.append(((grp, 32 * side + rest), 2 * grp + side))

    def z_of(self, slot):
        return lax.rem(self.z + NEAR[slot] % DEPTH, DEPTH)

    def at_slot(self, slot):
        return (self.grp, self.base + 2 * self.z_of(slot))


def answer(slot):
    return SLOT[-NEAR[slot] % DEPTH]


def remote(source, target, send_sem, recv_sem, peer):
    return pltpu.make_async_remote_copy(
        src_ref=source, dst_ref=target, send_sem=send_sem, recv_sem=recv_sem,
        device_id=peer, device_id_type=MESH,
    )


def await_bytes(ref, sem):
    pltpu.make_async_copy(ref, ref, sem).wait()


def kernel(
    total_rows,
    features_hbm, means_hbm, variances_hbm, logits_ref,
    fresh_means_ref, fresh_variances_ref, fresh_weights_ref, rows_ref,
    features, means, variances, tiles, arrived, table, weights, log_weights, inputs,
    exponents, peaks, totals, shares, tally,
    core_out, core_in, own, plane_in, z_out, z_in, back, spread,
    counts_z, counts_plane, counts_pair,
    load_sems, z_send, z_recv, plane_send, plane_recv, pair_send, pair_recv,
    rz_send, rz_recv, rplane_send, rplane_recv, rpair_send, rpair_recv,
    bz_send, bz_recv, bplane_send, bplane_recv, bpair_send, bpair_recv,
    count_send, count_recv,
):
    me = Place()
    local_rows = features.shape[0]
    barrier = pltpu.get_barrier_semaphore()
    greeted = [me.at_slot(slot) for slot in range(DEPTH - 1, 0, -1)]
    greeted += [peer for peer, _ in me.plane] + [me.sibling]
    for peer in greeted:
        pl.semaphore_signal(barrier, inc=1, device_id=peer, device_id_type=MESH)
    loads = [
        pltpu.make_async_copy(source, target, load_sems.at[index])
        for index, (source, target) in enumerate(
            ((means_hbm, means), (variances_hbm, variances), (features_hbm, features))
        )
    ]
    for load in loads:
        load.start()
    loads[0].wait()
    loads[1].wait()
    for index in range(8):
        source = means if index < 4 else variances
        column, row = (index // 2) % 2, index % 2
        tiles[index] = source[row * 8 : row * 8 + 8, column * 128 : column * 128 + 128]
    arrived[0] = tiles[me.grp]
    pl.semaphore_wait(barrier, len(greeted))

    def send_along_z(source, target, send_sem, recv_sem_of):
        for slot in range(DEPTH - 1, 0, -1):
            there = answer(slot)
            remote(
                source, target.at[there], send_sem, recv_sem_of(there), me.at_slot(slot)
            ).start()

    def pass_on(buffer, target, z_sems, send_sems, recv_sems, meanwhile=None):
        for hop, (first, count) in enumerate(HOPS):
            held = buffer.at[pl.ds(first, count)]
            if hop > 0:
                await_bytes(held, z_sems.at[hop])
            for k in range(count):
                target[me.core, me.chip, first + k] = buffer[first + k]
            for peer, _ in me.plane:
                remote(
                    held, target.at[me.core, me.chip, pl.ds(first, count)],
                    send_sems.at[hop], recv_sems.at[hop], peer,
                ).start()
            if hop == 0 and meanwhile is not None:
                meanwhile()

    def hops_of(index):
        return [hop for hop, (first, _) in enumerate(HOPS) if first // 4 == index]

    def await_hop(target, hop, sems):
        first, count = HOPS[hop]
        await_bytes(target.at[0, pl.ds(0, PEERS), pl.ds(first, count)], sems.at[hop])

    def across(target, index, send_sems, recv_sems):
        part = target.at[me.core, pl.ds(0, 16), pl.ds(4 * index, 4)]
        return remote(part, part, send_sems.at[index], recv_sems.at[index], me.sibling)

    send_along_z(arrived.at[0], arrived, z_send.at[0], lambda slot: z_recv.at[HOP_OF[slot]])

    def prepare(step, carry):
        at = pl.multiple_of(step * 128, 128)
        x = features[pl.ds(at, 128), :]
        values = x.astype(F32)
        squared = values * values
        high = squared.astype(BF16)
        low = (squared - high.astype(F32)).astype(BF16)
        for index, value in enumerate((high, low, high, x, x)):
            inputs[pl.ds(at, 128), index * WIDTH : index * WIDTH + WIDTH] = value
        return carry

    def prepare_all():
        logits = logits_ref[...]
        top = jnp.max(logits)
        normal = logits - top - jnp.log(jnp.sum(jnp.exp(logits - top)))
        for piece in range(8):
            wide = jnp.broadcast_to(normal[piece : piece + 1, :], (128, 128))
            log_weights[piece * 128 : piece * 128 + 128, :] = jnp.transpose(wide)
        loads[2].wait()
        lax.fori_loop(0, local_rows // 128, prepare, 0)

    pass_on(arrived, table, z_recv, plane_send, plane_recv, prepare_all)

    def natural(slot, half):
        return pl.multiple_of(512 * half + 32 * me.z_of(slot), 32)

    def make_weights(index):
        for v in range(2):
            for k in range(4):
                slot = 4 * index + k
                here = pl.ds(natural(slot, v), 32)
                penalties = []
                for h in range(2):
                    def load(kind, column):
                        chips = [2 * (4 * kind + 2 * column + r) + v for r in range(2)]
                        return jnp.concatenate([table[h, chip, slot] for chip in chips], axis=0)

                    row = 128 * v + 32 * k + 16 * h
                    rows = slice(row, row + 16)
                    penalty = None
                    for column in range(2):
                        mean, variance = load(0, column), load(1, column)
                        inverse = 1.0 / variance
                        square_part = -0.5 * inverse
                        linear_part = mean * inverse
                        term = jnp.log(variance) + mean * linear_part
                        penalty = term if penalty is None else penalty + term
                        square_high = square_part.astype(BF16)
                        square_low = (square_part - square_high.astype(F32)).astype(BF16)
                        linear_high = linear_part.astype(BF16)
                        linear_low = (linear_part - linear_high.astype(F32)).astype(BF16)
                        for at, value in enumerate(
                            (square_high, square_high, square_low, linear_high, linear_low)
                        ):
                            at = at * WIDTH + column * 128
                            weights[index, rows, at : at + 128] = value
                    penalties.append(jnp.sum(penalty, axis=1, keepdims=True))
                log_weights[here, :] = (
                    log_weights[here, :]
                    - 0.5 * jnp.concatenate(penalties, axis=0)
                    - 0.5 * WIDTH * math.log(2.0 * math.pi)
                )

    def make_scores(index):
        offset = jnp.concatenate(
            [log_weights[pl.ds(natural(4 * index + k, v), 32), :] for v in range(2) for k in range(4)],
            axis=0,
        )
        offset = jnp.concatenate([offset] * (BLOCK // 128), axis=1)

        def visit(step, carry):
            at = pl.multiple_of(step * BLOCK, BLOCK)
            raw = lax.dot_general(
                weights[index], inputs[pl.ds(at, BLOCK), :], (((1,), (1,)), ((), ())),
                preferred_element_type=F32,
            )
            raw = raw + offset
            best = jnp.max(raw, axis=0, keepdims=True)
            value = jnp.exp(raw - best)
            exponents[index, :, pl.ds(at, BLOCK)] = value
            peaks[index : index + 1, pl.ds(at, BLOCK)] = best
            totals[index : index + 1, pl.ds(at, BLOCK)] = jnp.sum(value, axis=0, keepdims=True)
            return carry

        lax.fori_loop(0, local_rows // BLOCK, visit, 0, unroll=True)

    for index in range(GROUPS):
        for hop in hops_of(index):
            await_hop(table, hop, plane_recv)
        copy = across(table, index, pair_send, pair_recv)
        copy.start()
        copy.wait_recv()
        make_weights(index)
        make_scores(index)

    best = jnp.max(peaks[0:GROUPS, :], axis=0, keepdims=True)
    factors = jnp.exp(peaks[0:GROUPS, :] - best)
    total = jnp.sum(totals[0:GROUPS, :] * factors, axis=0, keepdims=True)
    row_scores = (best + jnp.log(total)) / WIDTH
    for piece in range(local_rows // 128):
        rows_ref[piece : piece + 1, :] = row_scores[:, piece * 128 : piece * 128 + 128]
    totals[0:GROUPS, :] = factors / total

    def rpair_copy(index):
        return remote(
            core_out.at[index], core_in.at[index], rpair_send.at[index], rpair_recv.at[index],
            me.sibling,
        )

    def share(index):
        sums = None
        for step in range(local_rows // BLOCK):
            at = step * BLOCK
            rounded = (
                exponents[index, :, at : at + BLOCK] * totals[index : index + 1, at : at + BLOCK]
            ).astype(BF16)
            shares[index, :, at : at + BLOCK] = rounded
            wide = rounded.astype(F32)
            wide = wide[:, :128] + wide[:, 128:]
            sums = wide if sums is None else sums + wide
        for v in range(2):
            for k in range(4):
                row = 128 * v + 32 * k
                tally[pl.ds(natural(4 * index + k, v), 32), :] = sums[row : row + 32]

    def moments(index, half, target):
        result = jnp.dot(
            shares[index, pl.ds(pl.multiple_of(128 * half, 128), 128), :],
            inputs[:, 2 * WIDTH : 4 * WIDTH],
            preferred_element_type=F32,
        )
        for k in range(4):
            for chip in range(16):
                row, column = 32 * k + 8 * (chip // 4), 128 * (chip % 4)
                target[index, chip, k] = result[row : row + 8, column : column + 128]

    def to_plane(index):
        rpair_copy(index).wait_recv()
        own[index] = own[index] + core_in[index]
        for offset, (peer, chip) in enumerate(me.plane):
            remote(
                own.at[index, chip], plane_in.at[index, offset],
                rplane_send.at[index], rplane_recv.at[index], peer,
            ).start()

    for index in range(GROUPS - 1, -1, -1):
        share(index)
        moments(index, 1 - me.core, core_out)
        rpair_copy(index).start()
        if index < GROUPS - 1:
            to_plane(index + 1)
        moments(index, me.core, own)
    to_plane(0)

    for piece in range(8):
        line = jnp.sum(jnp.transpose(tally[piece * 128 : piece * 128 + 128, :]), axis=0, keepdims=True)
        counts_pair[0, piece : piece + 1, :] = line
    for slot in range(DEPTH - 1, 0, -1):
        remote(
            counts_pair.at[0], counts_z.at[me.z], count_send.at[0], count_recv.at[0],
            me.at_slot(slot),
        ).start()
    counts_z[me.z] = counts_pair[0]

    for index in range(GROUPS - 1, -1, -1):
        await_bytes(plane_in.at[index], rplane_recv.at[index])
        reduced = own[index, me.chip]
        for offset in range(PEERS):
            reduced = reduced + plane_in[index, offset]
        z_out[pl.ds(4 * index, 4)] = reduced
        for slot in range(4 * index + 3, max(4 * index, 1) - 1, -1):
            remote(
                z_out.at[slot], z_in.at[answer(slot)], rz_send.at[0], rz_recv.at[0],
                me.at_slot(slot),
            ).start()

    await_bytes(counts_z.at[pl.ds(0, DEPTH - 1)], count_recv.at[0])
    counted = counts_z[0]
    for index in range(1, DEPTH):
        counted = counted + counts_z[index]
    counts_plane[me.chip] = counted
    for peer, _ in me.plane:
        remote(
            counts_plane.at[me.chip], counts_plane.at[me.chip], count_send.at[1], count_recv.at[1],
            peer,
        ).start()

    await_bytes(z_in.at[pl.ds(1, DEPTH - 1)], rz_recv.at[0])
    final = z_out[0]
    for slot in range(1, DEPTH):
        final = final + z_in[slot]
    back[0] = final
    send_along_z(back.at[0], back, bz_send.at[0], lambda slot: bz_recv.at[HOP_OF[slot]])

    await_bytes(counts_plane.at[pl.ds(0, PEERS)], count_recv.at[1])
    counted = counts_plane[0]
    for index in range(1, 16):
        counted = counted + counts_plane[index]
    counts_pair[1] = counted
    pair = remote(
        counts_pair.at[1], counts_pair.at[2], count_send.at[2], count_recv.at[2], me.sibling
    )
    pair.start()

    pass_on(back, spread, bz_recv, bplane_send, bplane_recv)

    pair.wait()
    denominator = counts_pair[1] + counts_pair[2] + 1.0
    fresh_weights_ref[...] = jnp.log(denominator / total_rows)
    inverse = 1.0 / denominator
    for piece in range(8):
        wide = jnp.broadcast_to(inverse[piece : piece + 1, :], (128, 128))
        tally[piece * 128 : piece * 128 + 128, :] = jnp.transpose(wide)

    await_bytes(z_in.at[pl.ds(1, DEPTH - 1)], z_send.at[0])
    await_bytes(z_in.at[pl.ds(1, DEPTH - 1)], count_send.at[0])
    await_bytes(z_in.at[pl.ds(1, DEPTH - 1)], count_send.at[1])
    await_bytes(z_in.at[pl.ds(1, DEPTH - 1)], rz_send.at[0])
    await_bytes(z_in.at[pl.ds(1, DEPTH - 1)], bz_send.at[0])
    for hop in range(len(HOPS)):
        await_hop(table, hop, plane_send)
    for index in range(GROUPS):
        await_bytes(plane_in.at[index], rplane_send.at[index])
        across(table, index, pair_send, pair_recv).wait_send()
        rpair_copy(index).wait_send()

    def update(index):
        across(spread, index, bpair_send, bpair_recv).wait_recv()
        for h in range(2):
            for k in range(4):
                slot = 4 * index + k
                first = natural(slot, h)
                for r in range(4):
                    here = pl.ds(pl.multiple_of(first + 8 * r, 8), 8)
                    scale = tally[here, :]
                    for c in range(2):
                        squares, linears = spread[h, 4 * r + c, slot], spread[h, 4 * r + 2 + c, slot]
                        mean = linears * scale
                        fresh_means_ref[here, c * 128 : c * 128 + 128] = mean
                        fresh_variances_ref[here, c * 128 : c * 128 + 128] = (
                            (squares + 1.0) * scale - mean * mean + 0.01
                        )

    for index in range(GROUPS):
        for hop in hops_of(index):
            await_hop(spread, hop, bplane_recv)
        across(spread, index, bpair_send, bpair_recv).start()
        if index > 0:
            update(index - 1)
    update(GROUPS - 1)
    for hop in range(len(HOPS)):
        await_hop(spread, hop, bplane_send)
    for index in range(GROUPS):
        across(spread, index, bpair_send, bpair_recv).wait_send()


def iterate(features, means, variances, logits, total_rows):
    rows = features.shape[0]
    dma = pltpu.SemaphoreType.DMA
    hbm = pl.BlockSpec(memory_space=pl.ANY)
    vmem = pl.BlockSpec(memory_space=pltpu.VMEM)
    tile = (8, 128)
    hops = len(HOPS)
    return pl.pallas_call(
        functools.partial(kernel, total_rows),
        out_shape=(
            jax.ShapeDtypeStruct((COMPS, WIDTH), F32),
            jax.ShapeDtypeStruct((COMPS, WIDTH), F32),
            jax.ShapeDtypeStruct(tile, F32),
            jax.ShapeDtypeStruct((rows // 128, 128), F32),
        ),
        in_specs=[hbm, hbm, hbm, vmem],
        out_specs=(vmem,) * 4,
        scratch_shapes=[
            pltpu.VMEM((rows, WIDTH), BF16),
            pltpu.VMEM((16, WIDTH), F32),
            pltpu.VMEM((16, WIDTH), F32),
            pltpu.VMEM((8, *tile), F32),
            pltpu.VMEM((DEPTH, *tile), F32),
            pltpu.VMEM((2, 16, DEPTH, *tile), F32),
            pltpu.VMEM((GROUPS, 256, 5 * WIDTH), BF16),
            pltpu.VMEM((COMPS, 128), F32),
            pltpu.VMEM((rows, 5 * WIDTH), BF16),
            pltpu.VMEM((GROUPS, 256, rows), F32),
            pltpu.VMEM((8, rows), F32),
            pltpu.VMEM((8, rows), F32),
            pltpu.VMEM((GROUPS, 256, rows), BF16),
            pltpu.VMEM((COMPS, 128), F32),
            pltpu.VMEM((GROUPS, 16, 4, *tile), F32),
            pltpu.VMEM((GROUPS, 16, 4, *tile), F32),
            pltpu.VMEM((GROUPS, 16, 4, *tile), F32),
            pltpu.VMEM((GROUPS, PEERS, 4, *tile), F32),
            pltpu.VMEM((DEPTH, *tile), F32),
            pltpu.VMEM((DEPTH, *tile), F32),
            pltpu.VMEM((DEPTH, *tile), F32),
            pltpu.VMEM((2, 16, DEPTH, *tile), F32),
            pltpu.VMEM((DEPTH, *tile), F32),
            pltpu.VMEM((16, *tile), F32),
            pltpu.VMEM((3, *tile), F32),
            dma((3,)),
            dma((1,)), dma((hops,)), dma((hops,)), dma((hops,)), dma((GROUPS,)), dma((GROUPS,)),
            dma((1,)), dma((1,)), dma((GROUPS,)), dma((GROUPS,)), dma((GROUPS,)), dma((GROUPS,)),
            dma((1,)), dma((hops,)), dma((hops,)), dma((hops,)), dma((GROUPS,)), dma((GROUPS,)),
            dma((3,)), dma((3,)),
        ],
        compiler_params=pltpu.CompilerParams(
            collective_id=0, has_side_effects=True, vmem_limit_bytes=56 << 20
        ),
    )(features, means, variances, logits)


def on_device(features, means, variances, weight_logits):
    rows = features.shape[0]
    total_rows = float(rows * lax.axis_size("grp") * lax.axis_size("comp") + COMPS)
    fresh_means, fresh_variances, fresh_weights, row_scores = iterate(
        features, means, variances, weight_logits.reshape(8, 128), total_rows
    )
    return fresh_means, fresh_variances, fresh_weights.reshape(COMPS), row_scores.reshape(rows)


def solution(mesh):
    return jax.shard_map(
        on_device,
        mesh=mesh,
        in_specs=(P(("grp", "comp"), None), P("comp", None), P("comp", None), P()),
        out_specs=(P(), P(), P(), P(("grp", "comp"))),
        check_vma=False,
    )
```

```python
import functools
import math

import jax
import jax.numpy as jnp
from jax import lax
from jax.experimental import pallas as pl
from jax.experimental.pallas import tpu as pltpu
from jax.sharding import PartitionSpec as P

MESH = pl.DeviceIdType.MESH
BF16 = jnp.bfloat16
F32 = jnp.float32

COMPS, WIDTH = 1024, 256
DEPTH = 16
OFFSETS = sorted(
    ((dx, dy) for dx in range(4) for dy in range(4) if (dx, dy) != (0, 0)),
    key=lambda d: (-min(d[0], 4 - d[0]) - min(d[1], 4 - d[1]), d),
)
PEERS = len(OFFSETS)
NEAR = (0, 1, -1, 2, -2, 3, -3, 4, -4, 5, -5, 6, -6, 7, -7, 8)
SLOT = {step % DEPTH: slot for slot, step in enumerate(NEAR)}
HOPS = ((0, 1), (1, 3), (4, 2), (6, 2), (8, 2), (10, 2), (12, 2), (14, 2))
HOP_OF = {first + k: hop for hop, (first, count) in enumerate(HOPS) for k in range(count)}
GROUPS = 4
BLOCK = 256


class Place:
    def __init__(self):
        self.grp = lax.axis_index("grp")
        comp = lax.axis_index("comp")
        y, u = lax.div(self.grp, 2), lax.rem(self.grp, 2)
        v, rest = lax.div(comp, 32), lax.rem(comp, 32)
        self.z, self.core = lax.div(rest, 2), lax.rem(rest, 2)
        self.chip = 2 * self.grp + v
        self.sibling = (self.grp, comp + 1 - 2 * self.core)
        self.base = 32 * v + self.core
        x = 2 * u + v
        self.plane = []
        for dx, dy in OFFSETS:
            across, along = lax.rem(x + dx, 4), lax.rem(y + dy, 4)
            grp = 2 * along + lax.div(across, 2)
            side = lax.rem(across, 2)
            self.plane.append(((grp, 32 * side + rest), 2 * grp + side))

    def z_of(self, slot):
        return lax.rem(self.z + NEAR[slot] % DEPTH, DEPTH)

    def at_slot(self, slot):
        return (self.grp, self.base + 2 * self.z_of(slot))


def answer(slot):
    return SLOT[-NEAR[slot] % DEPTH]


def remote(source, target, send_sem, recv_sem, peer):
    return pltpu.make_async_remote_copy(
        src_ref=source, dst_ref=target, send_sem=send_sem, recv_sem=recv_sem,
        device_id=peer, device_id_type=MESH,
    )


def await_bytes(ref, sem):
    pltpu.make_async_copy(ref, ref, sem).wait()


def kernel(
    total_rows,
    features_hbm, means_hbm, variances_hbm, logits_ref,
    fresh_means_ref, fresh_variances_ref, fresh_weights_ref, rows_ref,
    features, means, variances, tiles, arrived, table, weights, log_weights, inputs,
    exponents, peaks, totals, shares, tally,
    core_out, core_in, own, plane_in, z_out, z_in, back, spread,
    counts_z, counts_plane, counts_pair,
    load_sems, z_send, z_recv, plane_send, plane_recv, pair_send, pair_recv,
    rz_send, rz_recv, rplane_send, rplane_recv, rpair_send, rpair_recv,
    bz_send, bz_recv, bplane_send, bplane_recv, bpair_send, bpair_recv,
    count_send, count_recv,
):
    me = Place()
    local_rows = features.shape[0]
    barrier = pltpu.get_barrier_semaphore()
    greeted = [me.at_slot(slot) for slot in range(DEPTH - 1, 0, -1)]
    greeted += [peer for peer, _ in me.plane] + [me.sibling]
    for peer in greeted:
        pl.semaphore_signal(barrier, inc=1, device_id=peer, device_id_type=MESH)
    loads = [
        pltpu.make_async_copy(source, target, load_sems.at[index])
        for index, (source, target) in enumerate(
            ((means_hbm, means), (variances_hbm, variances), (features_hbm, features))
        )
    ]
    for load in loads:
        load.start()
    loads[0].wait()
    loads[1].wait()
    for index in range(8):
        source = means if index < 4 else variances
        column, row = (index // 2) % 2, index % 2
        tiles[index] = source[row * 8 : row * 8 + 8, column * 128 : column * 128 + 128]
    arrived[0] = tiles[me.grp]
    pl.semaphore_wait(barrier, len(greeted))

    def send_along_z(source, target, send_sem, recv_sem_of):
        for slot in range(DEPTH - 1, 0, -1):
            there = answer(slot)
            remote(
                source, target.at[there], send_sem, recv_sem_of(there), me.at_slot(slot)
            ).start()

    def pass_on(buffer, target, z_sems, send_sems, recv_sems, meanwhile=None):
        for hop, (first, count) in enumerate(HOPS):
            held = buffer.at[pl.ds(first, count)]
            if hop > 0:
                await_bytes(held, z_sems.at[hop])
            for k in range(count):
                target[me.core, me.chip, first + k] = buffer[first + k]
            for peer, _ in me.plane:
                remote(
                    held, target.at[me.core, me.chip, pl.ds(first, count)],
                    send_sems.at[hop], recv_sems.at[hop], peer,
                ).start()
            if hop == 0 and meanwhile is not None:
                meanwhile()

    def hops_of(index):
        return [hop for hop, (first, _) in enumerate(HOPS) if first // 4 == index]

    def await_hop(target, hop, sems):
        first, count = HOPS[hop]
        await_bytes(target.at[0, pl.ds(0, PEERS), pl.ds(first, count)], sems.at[hop])

    def across(target, index, send_sems, recv_sems):
        part = target.at[me.core, pl.ds(0, 16), pl.ds(4 * index, 4)]
        return remote(part, part, send_sems.at[index], recv_sems.at[index], me.sibling)

    send_along_z(arrived.at[0], arrived, z_send.at[0], lambda slot: z_recv.at[HOP_OF[slot]])

    def prepare(step, carry):
        at = pl.multiple_of(step * 128, 128)
        x = features[pl.ds(at, 128), :]
        values = x.astype(F32)
        squared = values * values
        high = squared.astype(BF16)
        low = (squared - high.astype(F32)).astype(BF16)
        for index, value in enumerate((high, low, high, x, x)):
            inputs[pl.ds(at, 128), index * WIDTH : index * WIDTH + WIDTH] = value
        return carry

    def prepare_all():
        logits = logits_ref[...]
        top = jnp.max(logits)
        normal = logits - top - jnp.log(jnp.sum(jnp.exp(logits - top)))
        for piece in range(8):
            wide = jnp.broadcast_to(normal[piece : piece + 1, :], (128, 128))
            log_weights[piece * 128 : piece * 128 + 128, :] = jnp.transpose(wide)
        loads[2].wait()
        lax.fori_loop(0, local_rows // 128, prepare, 0)

    pass_on(arrived, table, z_recv, plane_send, plane_recv, prepare_all)

    def natural(slot, half):
        return pl.multiple_of(512 * half + 32 * me.z_of(slot), 32)

    def make_weights(index):
        for v in range(2):
            for k in range(4):
                slot = 4 * index + k
                here = pl.ds(natural(slot, v), 32)
                penalties = []
                for h in range(2):
                    def load(kind, column):
                        chips = [2 * (4 * kind + 2 * column + r) + v for r in range(2)]
                        return jnp.concatenate([table[h, chip, slot] for chip in chips], axis=0)

                    row = 128 * v + 32 * k + 16 * h
                    rows = slice(row, row + 16)
                    penalty = None
                    for column in range(2):
                        mean, variance = load(0, column), load(1, column)
                        inverse = 1.0 / variance
                        square_part = -0.5 * inverse
                        linear_part = mean * inverse
                        term = jnp.log(variance) + mean * linear_part
                        penalty = term if penalty is None else penalty + term
                        square_high = square_part.astype(BF16)
                        square_low = (square_part - square_high.astype(F32)).astype(BF16)
                        linear_high = linear_part.astype(BF16)
                        linear_low = (linear_part - linear_high.astype(F32)).astype(BF16)
                        for at, value in enumerate(
                            (square_high, square_high, square_low, linear_high, linear_low)
                        ):
                            at = at * WIDTH + column * 128
                            weights[index, rows, at : at + 128] = value
                    penalties.append(jnp.sum(penalty, axis=1, keepdims=True))
                log_weights[here, :] = (
                    log_weights[here, :]
                    - 0.5 * jnp.concatenate(penalties, axis=0)
                    - 0.5 * WIDTH * math.log(2.0 * math.pi)
                )

    def make_scores(index):
        offset = jnp.concatenate(
            [log_weights[pl.ds(natural(4 * index + k, v), 32), :] for v in range(2) for k in range(4)],
            axis=0,
        )
        offset = jnp.concatenate([offset] * (BLOCK // 128), axis=1)

        def visit(step, carry):
            at = pl.multiple_of(step * BLOCK, BLOCK)
            raw = lax.dot_general(
                weights[index], inputs[pl.ds(at, BLOCK), :], (((1,), (1,)), ((), ())),
                preferred_element_type=F32,
            )
            raw = raw + offset
            best = jnp.max(raw, axis=0, keepdims=True)
            value = jnp.exp(raw - best)
            exponents[index, :, pl.ds(at, BLOCK)] = value
            peaks[index : index + 1, pl.ds(at, BLOCK)] = best
            totals[index : index + 1, pl.ds(at, BLOCK)] = jnp.sum(value, axis=0, keepdims=True)
            return carry

        lax.fori_loop(0, local_rows // BLOCK, visit, 0, unroll=True)

    for index in range(GROUPS):
        for hop in hops_of(index):
            await_hop(table, hop, plane_recv)
        copy = across(table, index, pair_send, pair_recv)
        copy.start()
        copy.wait_recv()
        make_weights(index)
        make_scores(index)

    best = jnp.max(peaks[0:GROUPS, :], axis=0, keepdims=True)
    factors = jnp.exp(peaks[0:GROUPS, :] - best)
    total = jnp.sum(totals[0:GROUPS, :] * factors, axis=0, keepdims=True)
    row_scores = (best + jnp.log(total)) / WIDTH
    for piece in range(local_rows // 128):
        rows_ref[piece : piece + 1, :] = row_scores[:, piece * 128 : piece * 128 + 128]
    totals[0:GROUPS, :] = factors / total

    def rpair_copy(index):
        return remote(
            core_out.at[index], core_in.at[index], rpair_send.at[index], rpair_recv.at[index],
            me.sibling,
        )

    def share(index):
        sums = None
        for step in range(local_rows // BLOCK):
            at = step * BLOCK
            rounded = (
                exponents[index, :, at : at + BLOCK] * totals[index : index + 1, at : at + BLOCK]
            ).astype(BF16)
            shares[index, :, at : at + BLOCK] = rounded
            wide = rounded.astype(F32)
            wide = wide[:, :128] + wide[:, 128:]
            sums = wide if sums is None else sums + wide
        for v in range(2):
            for k in range(4):
                row = 128 * v + 32 * k
                tally[pl.ds(natural(4 * index + k, v), 32), :] = sums[row : row + 32]

    def moments(index, half, target):
        result = jnp.dot(
            shares[index, pl.ds(pl.multiple_of(128 * half, 128), 128), :],
            inputs[:, 2 * WIDTH : 4 * WIDTH],
            preferred_element_type=F32,
        )
        for k in range(4):
            for chip in range(16):
                row, column = 32 * k + 8 * (chip // 4), 128 * (chip % 4)
                target[index, chip, k] = result[row : row + 8, column : column + 128]

    def to_plane(index):
        rpair_copy(index).wait_recv()
        own[index] = own[index] + core_in[index]
        for offset, (peer, chip) in enumerate(me.plane):
            remote(
                own.at[index, chip], plane_in.at[index, offset],
                rplane_send.at[index], rplane_recv.at[index], peer,
            ).start()

    for index in range(GROUPS - 1, -1, -1):
        share(index)
        moments(index, 1 - me.core, core_out)
        rpair_copy(index).start()
        if index < GROUPS - 1:
            to_plane(index + 1)
        moments(index, me.core, own)
    to_plane(0)

    for piece in range(8):
        line = jnp.sum(jnp.transpose(tally[piece * 128 : piece * 128 + 128, :]), axis=0, keepdims=True)
        counts_pair[0, piece : piece + 1, :] = line
    for slot in range(DEPTH - 1, 0, -1):
        remote(
            counts_pair.at[0], counts_z.at[me.z], count_send.at[0], count_recv.at[0],
            me.at_slot(slot),
        ).start()
    counts_z[me.z] = counts_pair[0]

    for index in range(GROUPS - 1, -1, -1):
        await_bytes(plane_in.at[index], rplane_recv.at[index])
        reduced = own[index, me.chip]
        for offset in range(PEERS):
            reduced = reduced + plane_in[index, offset]
        z_out[pl.ds(4 * index, 4)] = reduced
        for slot in range(4 * index + 3, max(4 * index, 1) - 1, -1):
            remote(
                z_out.at[slot], z_in.at[answer(slot)], rz_send.at[0], rz_recv.at[0],
                me.at_slot(slot),
            ).start()

    await_bytes(counts_z.at[pl.ds(0, DEPTH - 1)], count_recv.at[0])
    counted = counts_z[0]
    for index in range(1, DEPTH):
        counted = counted + counts_z[index]
    counts_plane[me.chip] = counted
    for peer, _ in me.plane:
        remote(
            counts_plane.at[me.chip], counts_plane.at[me.chip], count_send.at[1], count_recv.at[1],
            peer,
        ).start()

    await_bytes(z_in.at[pl.ds(1, DEPTH - 1)], rz_recv.at[0])
    final = z_out[0]
    for slot in range(1, DEPTH):
        final = final + z_in[slot]
    back[0] = final
    send_along_z(back.at[0], back, bz_send.at[0], lambda slot: bz_recv.at[HOP_OF[slot]])

    await_bytes(counts_plane.at[pl.ds(0, PEERS)], count_recv.at[1])
    counted = counts_plane[0]
    for index in range(1, 16):
        counted = counted + counts_plane[index]
    counts_pair[1] = counted
    pair = remote(
        counts_pair.at[1], counts_pair.at[2], count_send.at[2], count_recv.at[2], me.sibling
    )
    pair.start()

    pass_on(back, spread, bz_recv, bplane_send, bplane_recv)

    pair.wait()
    denominator = counts_pair[1] + counts_pair[2] + 1.0
    fresh_weights_ref[...] = jnp.log(denominator / total_rows)
    inverse = 1.0 / denominator
    for piece in range(8):
        wide = jnp.broadcast_to(inverse[piece : piece + 1, :], (128, 128))
        tally[piece * 128 : piece * 128 + 128, :] = jnp.transpose(wide)

    await_bytes(z_in.at[pl.ds(1, DEPTH - 1)], z_send.at[0])
    await_bytes(z_in.at[pl.ds(1, DEPTH - 1)], count_send.at[0])
    await_bytes(z_in.at[pl.ds(1, DEPTH - 1)], count_send.at[1])
    await_bytes(z_in.at[pl.ds(1, DEPTH - 1)], rz_send.at[0])
    await_bytes(z_in.at[pl.ds(1, DEPTH - 1)], bz_send.at[0])
    for hop in range(len(HOPS)):
        await_hop(table, hop, plane_send)
    for index in range(GROUPS):
        await_bytes(plane_in.at[index], rplane_send.at[index])
        across(table, index, pair_send, pair_recv).wait_send()
        rpair_copy(index).wait_send()

    def update(index):
        across(spread, index, bpair_send, bpair_recv).wait_recv()
        for h in range(2):
            for k in range(4):
                slot = 4 * index + k
                first = natural(slot, h)
                for r in range(4):
                    here = pl.ds(pl.multiple_of(first + 8 * r, 8), 8)
                    scale = tally[here, :]
                    for c in range(2):
                        squares, linears = spread[h, 4 * r + c, slot], spread[h, 4 * r + 2 + c, slot]
                        mean = linears * scale
                        fresh_means_ref[here, c * 128 : c * 128 + 128] = mean
                        fresh_variances_ref[here, c * 128 : c * 128 + 128] = (
                            (squares + 1.0) * scale - mean * mean + 0.01
                        )

    for index in range(GROUPS):
        for hop in hops_of(index):
            await_hop(spread, hop, bplane_recv)
        across(spread, index, bpair_send, bpair_recv).start()
        if index > 0:
            update(index - 1)
    update(GROUPS - 1)
    for hop in range(len(HOPS)):
        await_hop(spread, hop, bplane_send)
    for index in range(GROUPS):
        across(spread, index, bpair_send, bpair_recv).wait_send()


def iterate(features, means, variances, logits, total_rows):
    rows = features.shape[0]
    dma = pltpu.SemaphoreType.DMA
    hbm = pl.BlockSpec(memory_space=pl.ANY)
    vmem = pl.BlockSpec(memory_space=pltpu.VMEM)
    tile = (8, 128)
    hops = len(HOPS)
    return pl.pallas_call(
        functools.partial(kernel, total_rows),
        out_shape=(
            jax.ShapeDtypeStruct((COMPS, WIDTH), F32),
            jax.ShapeDtypeStruct((COMPS, WIDTH), F32),
            jax.ShapeDtypeStruct(tile, F32),
            jax.ShapeDtypeStruct((rows // 128, 128), F32),
        ),
        in_specs=[hbm, hbm, hbm, vmem],
        out_specs=(vmem,) * 4,
        scratch_shapes=[
            pltpu.VMEM((rows, WIDTH), BF16),
            pltpu.VMEM((16, WIDTH), F32),
            pltpu.VMEM((16, WIDTH), F32),
            pltpu.VMEM((8, *tile), F32),
            pltpu.VMEM((DEPTH, *tile), F32),
            pltpu.VMEM((2, 16, DEPTH, *tile), F32),
            pltpu.VMEM((GROUPS, 256, 5 * WIDTH), BF16),
            pltpu.VMEM((COMPS, 128), F32),
            pltpu.VMEM((rows, 5 * WIDTH), BF16),
            pltpu.VMEM((GROUPS, 256, rows), F32),
            pltpu.VMEM((8, rows), F32),
            pltpu.VMEM((8, rows), F32),
            pltpu.VMEM((GROUPS, 256, rows), BF16),
            pltpu.VMEM((COMPS, 128), F32),
            pltpu.VMEM((GROUPS, 16, 4, *tile), F32),
            pltpu.VMEM((GROUPS, 16, 4, *tile), F32),
            pltpu.VMEM((GROUPS, 16, 4, *tile), F32),
            pltpu.VMEM((GROUPS, PEERS, 4, *tile), F32),
            pltpu.VMEM((DEPTH, *tile), F32),
            pltpu.VMEM((DEPTH, *tile), F32),
            pltpu.VMEM((DEPTH, *tile), F32),
            pltpu.VMEM((2, 16, DEPTH, *tile), F32),
            pltpu.VMEM((DEPTH, *tile), F32),
            pltpu.VMEM((16, *tile), F32),
            pltpu.VMEM((3, *tile), F32),
            dma((3,)),
            dma((1,)), dma((hops,)), dma((hops,)), dma((hops,)), dma((GROUPS,)), dma((GROUPS,)),
            dma((1,)), dma((1,)), dma((GROUPS,)), dma((GROUPS,)), dma((GROUPS,)), dma((GROUPS,)),
            dma((1,)), dma((hops,)), dma((hops,)), dma((hops,)), dma((GROUPS,)), dma((GROUPS,)),
            dma((3,)), dma((3,)),
        ],
        compiler_params=pltpu.CompilerParams(
            collective_id=0, has_side_effects=True, vmem_limit_bytes=56 << 20
        ),
    )(features, means, variances, logits)


def hand_on_kernel(*refs):
    sources, targets, holds, sems = refs[:4], refs[4:8], refs[8:12], refs[12]
    loads, stores = [], []
    for source, target, hold in zip(sources, targets, holds):
        pieces = 4 if source.shape[0] == COMPS else 1
        size = source.shape[0] // pieces
        for piece in range(pieces):
            part = pl.ds(piece * size, size)
            at = len(loads)
            loads.append(pltpu.make_async_copy(source.at[part], hold.at[part], sems.at[0, at]))
            stores.append(pltpu.make_async_copy(hold.at[part], target.at[part], sems.at[1, at]))
    for load in loads:
        load.start()
    for load, store in zip(loads, stores):
        load.wait()
        store.start()
    for store in stores:
        store.wait()


def hand_on(*arrays):
    anywhere = pl.BlockSpec(memory_space=pl.ANY)
    return pl.pallas_call(
        hand_on_kernel,
        out_shape=tuple(jax.ShapeDtypeStruct(a.shape, a.dtype) for a in arrays),
        in_specs=[anywhere] * 4,
        out_specs=(anywhere,) * 4,
        scratch_shapes=[
            *(pltpu.VMEM(a.shape, a.dtype) for a in arrays),
            pltpu.SemaphoreType.DMA((2, 10)),
        ],
    )(*arrays)


def on_device(features, means, variances, weight_logits):
    rows = features.shape[0]
    total_rows = float(rows * lax.axis_size("grp") * lax.axis_size("comp") + COMPS)
    fresh_means, fresh_variances, fresh_weights, row_scores = hand_on(
        *iterate(features, means, variances, weight_logits.reshape(8, 128), total_rows)
    )
    return fresh_means, fresh_variances, fresh_weights.reshape(COMPS), row_scores.reshape(rows)


def solution(mesh):
    return jax.shard_map(
        on_device,
        mesh=mesh,
        in_specs=(P(("grp", "comp"), None), P("comp", None), P("comp", None), P()),
        out_specs=(P(), P(), P(), P(("grp", "comp"))),
        check_vma=False,
    )
```

```python
import functools
import math

import jax
import jax.numpy as jnp
from jax import lax
from jax.experimental import pallas as pl
from jax.experimental.pallas import tpu as pltpu
from jax.sharding import PartitionSpec as P

MESH = pl.DeviceIdType.MESH
BF16 = jnp.bfloat16
F32 = jnp.float32

COMPS, WIDTH = 1024, 256
DEPTH = 16
OFFSETS = sorted(
    ((dx, dy) for dx in range(4) for dy in range(4) if (dx, dy) != (0, 0)),
    key=lambda d: (-min(d[0], 4 - d[0]) - min(d[1], 4 - d[1]), d),
)
PEERS = len(OFFSETS)
NEAR = (0, 1, -1, 2, -2, 3, -3, 4, -4, 5, -5, 6, -6, 7, -7, 8)
SLOT = {step % DEPTH: slot for slot, step in enumerate(NEAR)}
HOPS = ((0, 1), (1, 3), (4, 2), (6, 2), (8, 2), (10, 2), (12, 2), (14, 2))
HOP_OF = {first + k: hop for hop, (first, count) in enumerate(HOPS) for k in range(count)}
GROUPS = 4
BLOCK = 256


class Place:
    def __init__(self):
        self.grp = lax.axis_index("grp")
        comp = lax.axis_index("comp")
        y, u = lax.div(self.grp, 2), lax.rem(self.grp, 2)
        v, rest = lax.div(comp, 32), lax.rem(comp, 32)
        self.z, self.core = lax.div(rest, 2), lax.rem(rest, 2)
        self.chip = 2 * self.grp + v
        self.sibling = (self.grp, comp + 1 - 2 * self.core)
        self.base = 32 * v + self.core
        x = 2 * u + v
        self.plane = []
        for dx, dy in OFFSETS:
            across, along = lax.rem(x + dx, 4), lax.rem(y + dy, 4)
            grp = 2 * along + lax.div(across, 2)
            side = lax.rem(across, 2)
            self.plane.append(((grp, 32 * side + rest), 2 * grp + side))

    def z_of(self, slot):
        return lax.rem(self.z + NEAR[slot] % DEPTH, DEPTH)

    def at_slot(self, slot):
        return (self.grp, self.base + 2 * self.z_of(slot))


def answer(slot):
    return SLOT[-NEAR[slot] % DEPTH]


def remote(source, target, send_sem, recv_sem, peer):
    return pltpu.make_async_remote_copy(
        src_ref=source, dst_ref=target, send_sem=send_sem, recv_sem=recv_sem,
        device_id=peer, device_id_type=MESH,
    )


def await_bytes(ref, sem):
    pltpu.make_async_copy(ref, ref, sem).wait()


def kernel(
    total_rows,
    features_hbm, means_hbm, variances_hbm, logits_ref,
    fresh_means_ref, fresh_variances_ref, fresh_weights_ref, rows_ref,
    features, means, variances, tiles, arrived, table, weights, log_weights, inputs,
    exponents, peaks, totals, shares, tally,
    both, core_in, plane_in, z_out, z_in, back, spread,
    counts_z, counts_plane, counts_pair,
    load_sems, z_send, z_recv, plane_send, plane_recv, pair_send, pair_recv,
    rz_send, rz_recv, rplane_send, rplane_recv, rpair_send, rpair_recv,
    bz_send, bz_recv, bplane_send, bplane_recv, bpair_send, bpair_recv,
    count_send, count_recv,
):
    me = Place()
    local_rows = features.shape[0]
    barrier = pltpu.get_barrier_semaphore()
    greeted = [me.at_slot(slot) for slot in range(DEPTH - 1, 0, -1)]
    greeted += [peer for peer, _ in me.plane] + [me.sibling]
    for peer in greeted:
        pl.semaphore_signal(barrier, inc=1, device_id=peer, device_id_type=MESH)
    loads = [
        pltpu.make_async_copy(source, target, load_sems.at[index])
        for index, (source, target) in enumerate(
            ((means_hbm, means), (variances_hbm, variances), (features_hbm, features))
        )
    ]
    for load in loads:
        load.start()
    loads[0].wait()
    loads[1].wait()
    for index in range(8):
        source = means if index < 4 else variances
        column, row = (index // 2) % 2, index % 2
        tiles[index] = source[row * 8 : row * 8 + 8, column * 128 : column * 128 + 128]
    arrived[0] = tiles[me.grp]
    pl.semaphore_wait(barrier, len(greeted))

    def send_along_z(source, target, send_sem, recv_sem_of):
        for slot in range(DEPTH - 1, 0, -1):
            there = answer(slot)
            remote(
                source, target.at[there], send_sem, recv_sem_of(there), me.at_slot(slot)
            ).start()

    def pass_on(buffer, target, z_sems, send_sems, recv_sems, meanwhile=None):
        for hop, (first, count) in enumerate(HOPS):
            held = buffer.at[pl.ds(first, count)]
            if hop > 0:
                await_bytes(held, z_sems.at[hop])
            for k in range(count):
                target[me.core, me.chip, first + k] = buffer[first + k]
            for peer, _ in me.plane:
                remote(
                    held, target.at[me.core, me.chip, pl.ds(first, count)],
                    send_sems.at[hop], recv_sems.at[hop], peer,
                ).start()
            if hop == 0 and meanwhile is not None:
                meanwhile()

    def hops_of(index):
        return [hop for hop, (first, _) in enumerate(HOPS) if first // 4 == index]

    def await_hop(target, hop, sems):
        first, count = HOPS[hop]
        await_bytes(target.at[0, pl.ds(0, PEERS), pl.ds(first, count)], sems.at[hop])

    def across(target, index, send_sems, recv_sems):
        part = target.at[me.core, pl.ds(0, 16), pl.ds(4 * index, 4)]
        return remote(part, part, send_sems.at[index], recv_sems.at[index], me.sibling)

    send_along_z(arrived.at[0], arrived, z_send.at[0], lambda slot: z_recv.at[HOP_OF[slot]])

    def prepare(step, carry):
        at = pl.multiple_of(step * 128, 128)
        x = features[pl.ds(at, 128), :]
        values = x.astype(F32)
        squared = values * values
        high = squared.astype(BF16)
        low = (squared - high.astype(F32)).astype(BF16)
        for index, value in enumerate((high, low, high, x, x)):
            inputs[pl.ds(at, 128), index * WIDTH : index * WIDTH + WIDTH] = value
        return carry

    def prepare_all():
        logits = logits_ref[...]
        top = jnp.max(logits)
        normal = logits - top - jnp.log(jnp.sum(jnp.exp(logits - top)))
        for piece in range(8):
            wide = jnp.broadcast_to(normal[piece : piece + 1, :], (128, 128))
            log_weights[piece * 128 : piece * 128 + 128, :] = jnp.transpose(wide)
        loads[2].wait()
        lax.fori_loop(0, local_rows // 128, prepare, 0)

    pass_on(arrived, table, z_recv, plane_send, plane_recv, prepare_all)

    def natural(slot, half):
        return pl.multiple_of(512 * half + 32 * me.z_of(slot), 32)

    def make_weights(index):
        for v in range(2):
            for k in range(4):
                slot = 4 * index + k
                here = pl.ds(natural(slot, v), 32)
                penalties = []
                for h in range(2):
                    def load(kind, column):
                        chips = [2 * (4 * kind + 2 * column + r) + v for r in range(2)]
                        return jnp.concatenate([table[h, chip, slot] for chip in chips], axis=0)

                    row = 128 * v + 32 * k + 16 * h
                    rows = slice(row, row + 16)
                    penalty = None
                    for column in range(2):
                        mean, variance = load(0, column), load(1, column)
                        inverse = 1.0 / variance
                        square_part = -0.5 * inverse
                        linear_part = mean * inverse
                        term = jnp.log(variance) + mean * linear_part
                        penalty = term if penalty is None else penalty + term
                        square_high = square_part.astype(BF16)
                        square_low = (square_part - square_high.astype(F32)).astype(BF16)
                        linear_high = linear_part.astype(BF16)
                        linear_low = (linear_part - linear_high.astype(F32)).astype(BF16)
                        for at, value in enumerate(
                            (square_high, square_high, square_low, linear_high, linear_low)
                        ):
                            at = at * WIDTH + column * 128
                            weights[index, rows, at : at + 128] = value
                    penalties.append(jnp.sum(penalty, axis=1, keepdims=True))
                log_weights[here, :] = (
                    log_weights[here, :]
                    - 0.5 * jnp.concatenate(penalties, axis=0)
                    - 0.5 * WIDTH * math.log(2.0 * math.pi)
                )

    def make_scores(index):
        offset = jnp.concatenate(
            [log_weights[pl.ds(natural(4 * index + k, v), 32), :] for v in range(2) for k in range(4)],
            axis=0,
        )
        offset = jnp.concatenate([offset] * (BLOCK // 128), axis=1)

        def visit(step, carry):
            at = pl.multiple_of(step * BLOCK, BLOCK)
            raw = lax.dot_general(
                weights[index], inputs[pl.ds(at, BLOCK), :], (((1,), (1,)), ((), ())),
                preferred_element_type=F32,
            )
            raw = raw + offset
            best = jnp.max(raw, axis=0, keepdims=True)
            value = jnp.exp(raw - best)
            exponents[index, :, pl.ds(at, BLOCK)] = value
            peaks[index : index + 1, pl.ds(at, BLOCK)] = best
            totals[index : index + 1, pl.ds(at, BLOCK)] = jnp.sum(value, axis=0, keepdims=True)
            return carry

        lax.fori_loop(0, local_rows // BLOCK, visit, 0, unroll=True)

    def pair_up(index):
        for hop in hops_of(index):
            await_hop(table, hop, plane_recv)
        across(table, index, pair_send, pair_recv).start()

    pair_up(0)
    for index in range(GROUPS):
        across(table, index, pair_send, pair_recv).wait_recv()
        make_weights(index)
        if index + 1 < GROUPS:
            pair_up(index + 1)
        make_scores(index)

    best = jnp.max(peaks[0:GROUPS, :], axis=0, keepdims=True)
    factors = jnp.exp(peaks[0:GROUPS, :] - best)
    total = jnp.sum(totals[0:GROUPS, :] * factors, axis=0, keepdims=True)
    peaks[7:8, :] = best
    totals[7:8, :] = total
    totals[0:GROUPS, :] = factors / total

    def rpair_copy(index):
        return remote(
            both.at[index, 1 - me.core], core_in.at[index], rpair_send.at[index], rpair_recv.at[index],
            me.sibling,
        )

    def share(index):
        sums = None
        for step in range(local_rows // BLOCK):
            at = step * BLOCK
            rounded = (
                exponents[index, :, at : at + BLOCK] * totals[index : index + 1, at : at + BLOCK]
            ).astype(BF16)
            shares[index, :, at : at + BLOCK] = rounded
            wide = rounded.astype(F32)
            wide = wide[:, :128] + wide[:, 128:]
            sums = wide if sums is None else sums + wide
        for v in range(2):
            for k in range(4):
                row = 128 * v + 32 * k
                tally[pl.ds(natural(4 * index + k, v), 32), :] = sums[row : row + 32]

    def moments(index):
        result = jnp.dot(
            shares[index], inputs[:, 2 * WIDTH : 4 * WIDTH], preferred_element_type=F32
        )
        for v in range(2):
            for k in range(4):
                for chip in range(16):
                    row, column = 128 * v + 32 * k + 8 * (chip // 4), 128 * (chip % 4)
                    both[index, v, chip, k] = result[row : row + 8, column : column + 128]

    def to_plane(index):
        rpair_copy(index).wait_recv()
        both[index, me.core] = both[index, me.core] + core_in[index]
        for offset, (peer, chip) in enumerate(me.plane):
            remote(
                both.at[index, me.core, chip], plane_in.at[index, offset],
                rplane_send.at[index], rplane_recv.at[index], peer,
            ).start()

    for index in range(GROUPS - 1, -1, -1):
        share(index)
        moments(index)
        rpair_copy(index).start()
        if index < GROUPS - 1:
            to_plane(index + 1)
    to_plane(0)

    row_scores = (peaks[7:8, :] + jnp.log(totals[7:8, :])) / WIDTH
    for piece in range(local_rows // 128):
        rows_ref[piece : piece + 1, :] = row_scores[:, piece * 128 : piece * 128 + 128]

    for piece in range(8):
        line = jnp.sum(jnp.transpose(tally[piece * 128 : piece * 128 + 128, :]), axis=0, keepdims=True)
        counts_pair[0, piece : piece + 1, :] = line
    for slot in range(DEPTH - 1, 0, -1):
        remote(
            counts_pair.at[0], counts_z.at[me.z], count_send.at[0], count_recv.at[0],
            me.at_slot(slot),
        ).start()
    counts_z[me.z] = counts_pair[0]

    for index in range(GROUPS - 1, -1, -1):
        await_bytes(plane_in.at[index], rplane_recv.at[index])
        reduced = both[index, me.core, me.chip]
        for offset in range(PEERS):
            reduced = reduced + plane_in[index, offset]
        z_out[pl.ds(4 * index, 4)] = reduced
        for slot in range(4 * index + 3, max(4 * index, 1) - 1, -1):
            remote(
                z_out.at[slot], z_in.at[answer(slot)], rz_send.at[0], rz_recv.at[0],
                me.at_slot(slot),
            ).start()

    await_bytes(counts_z.at[pl.ds(0, DEPTH - 1)], count_recv.at[0])
    counted = counts_z[0]
    for index in range(1, DEPTH):
        counted = counted + counts_z[index]
    counts_plane[me.chip] = counted
    for peer, _ in me.plane:
        remote(
            counts_plane.at[me.chip], counts_plane.at[me.chip], count_send.at[1], count_recv.at[1],
            peer,
        ).start()

    await_bytes(z_in.at[pl.ds(1, DEPTH - 1)], rz_recv.at[0])
    final = z_out[0]
    for slot in range(1, DEPTH):
        final = final + z_in[slot]
    back[0] = final
    send_along_z(back.at[0], back, bz_send.at[0], lambda slot: bz_recv.at[HOP_OF[slot]])

    await_bytes(counts_plane.at[pl.ds(0, PEERS)], count_recv.at[1])
    counted = counts_plane[0]
    for index in range(1, 16):
        counted = counted + counts_plane[index]
    counts_pair[1] = counted
    pair = remote(
        counts_pair.at[1], counts_pair.at[2], count_send.at[2], count_recv.at[2], me.sibling
    )
    pair.start()

    pass_on(back, spread, bz_recv, bplane_send, bplane_recv)

    pair.wait()
    denominator = counts_pair[1] + counts_pair[2] + 1.0
    fresh_weights_ref[...] = jnp.log(denominator / total_rows)
    inverse = 1.0 / denominator
    for piece in range(8):
        wide = jnp.broadcast_to(inverse[piece : piece + 1, :], (128, 128))
        tally[piece * 128 : piece * 128 + 128, :] = jnp.transpose(wide)

    await_bytes(z_in.at[pl.ds(1, DEPTH - 1)], z_send.at[0])
    await_bytes(z_in.at[pl.ds(1, DEPTH - 1)], count_send.at[0])
    await_bytes(z_in.at[pl.ds(1, DEPTH - 1)], count_send.at[1])
    await_bytes(z_in.at[pl.ds(1, DEPTH - 1)], rz_send.at[0])
    await_bytes(z_in.at[pl.ds(1, DEPTH - 1)], bz_send.at[0])
    for hop in range(len(HOPS)):
        await_hop(table, hop, plane_send)
    for index in range(GROUPS):
        await_bytes(plane_in.at[index], rplane_send.at[index])
        across(table, index, pair_send, pair_recv).wait_send()
        rpair_copy(index).wait_send()

    def update(index):
        across(spread, index, bpair_send, bpair_recv).wait_recv()
        for h in range(2):
            for k in range(4):
                slot = 4 * index + k
                first = natural(slot, h)
                for r in range(4):
                    here = pl.ds(pl.multiple_of(first + 8 * r, 8), 8)
                    scale = tally[here, :]
                    for c in range(2):
                        squares, linears = spread[h, 4 * r + c, slot], spread[h, 4 * r + 2 + c, slot]
                        mean = linears * scale
                        fresh_means_ref[here, c * 128 : c * 128 + 128] = mean
                        fresh_variances_ref[here, c * 128 : c * 128 + 128] = (
                            (squares + 1.0) * scale - mean * mean + 0.01
                        )

    for index in range(GROUPS):
        for hop in hops_of(index):
            await_hop(spread, hop, bplane_recv)
        across(spread, index, bpair_send, bpair_recv).start()
        if index > 0:
            update(index - 1)
    update(GROUPS - 1)
    for hop in range(len(HOPS)):
        await_hop(spread, hop, bplane_send)
    for index in range(GROUPS):
        across(spread, index, bpair_send, bpair_recv).wait_send()


def iterate(features, means, variances, logits, total_rows):
    rows = features.shape[0]
    dma = pltpu.SemaphoreType.DMA
    hbm = pl.BlockSpec(memory_space=pl.ANY)
    vmem = pl.BlockSpec(memory_space=pltpu.VMEM)
    tile = (8, 128)
    hops = len(HOPS)
    return pl.pallas_call(
        functools.partial(kernel, total_rows),
        out_shape=(
            jax.ShapeDtypeStruct((COMPS, WIDTH), F32),
            jax.ShapeDtypeStruct((COMPS, WIDTH), F32),
            jax.ShapeDtypeStruct(tile, F32),
            jax.ShapeDtypeStruct((rows // 128, 128), F32),
        ),
        in_specs=[hbm, hbm, hbm, vmem],
        out_specs=(vmem,) * 4,
        scratch_shapes=[
            pltpu.VMEM((rows, WIDTH), BF16),
            pltpu.VMEM((16, WIDTH), F32),
            pltpu.VMEM((16, WIDTH), F32),
            pltpu.VMEM((8, *tile), F32),
            pltpu.VMEM((DEPTH, *tile), F32),
            pltpu.VMEM((2, 16, DEPTH, *tile), F32),
            pltpu.VMEM((GROUPS, 256, 5 * WIDTH), BF16),
            pltpu.VMEM((COMPS, 128), F32),
            pltpu.VMEM((rows, 5 * WIDTH), BF16),
            pltpu.VMEM((GROUPS, 256, rows), F32),
            pltpu.VMEM((8, rows), F32),
            pltpu.VMEM((8, rows), F32),
            pltpu.VMEM((GROUPS, 256, rows), BF16),
            pltpu.VMEM((COMPS, 128), F32),
            pltpu.VMEM((GROUPS, 2, 16, 4, *tile), F32),
            pltpu.VMEM((GROUPS, 16, 4, *tile), F32),
            pltpu.VMEM((GROUPS, PEERS, 4, *tile), F32),
            pltpu.VMEM((DEPTH, *tile), F32),
            pltpu.VMEM((DEPTH, *tile), F32),
            pltpu.VMEM((DEPTH, *tile), F32),
            pltpu.VMEM((2, 16, DEPTH, *tile), F32),
            pltpu.VMEM((DEPTH, *tile), F32),
            pltpu.VMEM((16, *tile), F32),
            pltpu.VMEM((3, *tile), F32),
            dma((3,)),
            dma((1,)), dma((hops,)), dma((hops,)), dma((hops,)), dma((GROUPS,)), dma((GROUPS,)),
            dma((1,)), dma((1,)), dma((GROUPS,)), dma((GROUPS,)), dma((GROUPS,)), dma((GROUPS,)),
            dma((1,)), dma((hops,)), dma((hops,)), dma((hops,)), dma((GROUPS,)), dma((GROUPS,)),
            dma((3,)), dma((3,)),
        ],
        compiler_params=pltpu.CompilerParams(
            collective_id=0, has_side_effects=True, vmem_limit_bytes=56 << 20
        ),
    )(features, means, variances, logits)


def hand_on_kernel(*refs):
    sources, targets, holds, sems = refs[:4], refs[4:8], refs[8:12], refs[12]
    loads, stores = [], []
    for source, target, hold in zip(sources, targets, holds):
        pieces = 4 if source.shape[0] == COMPS else 1
        size = source.shape[0] // pieces
        for piece in range(pieces):
            part = pl.ds(piece * size, size)
            at = len(loads)
            loads.append(pltpu.make_async_copy(source.at[part], hold.at[part], sems.at[0, at]))
            stores.append(pltpu.make_async_copy(hold.at[part], target.at[part], sems.at[1, at]))
    for load in loads:
        load.start()
    for load, store in zip(loads, stores):
        load.wait()
        store.start()
    for store in stores:
        store.wait()


def hand_on(*arrays):
    anywhere = pl.BlockSpec(memory_space=pl.ANY)
    return pl.pallas_call(
        hand_on_kernel,
        out_shape=tuple(jax.ShapeDtypeStruct(a.shape, a.dtype) for a in arrays),
        in_specs=[anywhere] * 4,
        out_specs=(anywhere,) * 4,
        scratch_shapes=[
            *(pltpu.VMEM(a.shape, a.dtype) for a in arrays),
            pltpu.SemaphoreType.DMA((2, 10)),
        ],
    )(*arrays)


def on_device(features, means, variances, weight_logits):
    rows = features.shape[0]
    total_rows = float(rows * lax.axis_size("grp") * lax.axis_size("comp") + COMPS)
    fresh_means, fresh_variances, fresh_weights, row_scores = hand_on(
        *iterate(features, means, variances, weight_logits.reshape(8, 128), total_rows)
    )
    return fresh_means, fresh_variances, fresh_weights.reshape(COMPS), row_scores.reshape(rows)


def solution(mesh):
    return jax.shard_map(
        on_device,
        mesh=mesh,
        in_specs=(P(("grp", "comp"), None), P("comp", None), P("comp", None), P()),
        out_specs=(P(), P(), P(), P(("grp", "comp"))),
        check_vma=False,
    )
```
